32 devices in a mesh: slab: 8 (over z, y), rays: 4 (over x, core).
Axes of the slice: x: 2, y: 2, z: 4, core: 2. Of those that a mesh axis runs over, the one named last changes fastest.
Arguments:
- geometry: float32 [6, 4, 128], P(None, 'rays'), may hold values from -1 to 1
- entry: int32 [8, 4, 128], P('slab', 'rays'), may hold values from 0 to 63
- counts: int32 [8, 4, 128], P('slab', 'rays'), may hold values from 0 to 8
- targets: float32 [3, 4, 128], P(None, 'rays', 'slab'), may hold values from 0 to 1
- w_in: float32 [8, 256, 256], P('slab'), may hold values from -0.375 to 0.375
- w_mid: float32 [8, 2, 256, 256], P('slab'), may hold values from -0.375 to 0.375
- w_out: float32 [8, 4, 256], P('slab'), may hold values from -0.375 to 0.375
- b_hid: float32 [8, 3, 256], P('slab'), may hold values from -3 to 3
- b_out: float32 [8, 4], P('slab'), may hold values from -3 to 3
- freqs: float32 [8, 3, 128], P('slab'), may hold values from -3 to 3
Outputs:
- pixels: float32 [3, 4, 128], P(None, 'rays', 'slab')
- grad_in: float32 [8, 256, 256], P('slab')
- grad_mid: float32 [8, 2, 256, 256], P('slab')
- grad_out: float32 [8, 4, 256], P('slab')
- grad_hid: float32 [8, 3, 256], P('slab')
- grad_bout: float32 [8, 4], P('slab')
The draws below stay inside these ranges and needn't reach their ends.
Inputs may be any that keep to these rules, and one draw needn't show every extreme that they name: `entry`: the index of a ray's first sample in a slab. `counts`: how many of the 8 slots of a ray lie inside a slab; 0 where the ray misses it.
All inputs are finite; a program needn't handle non-finite values.
Results may differ from the reference program's by a relative error of at most 0.0003.
Values sent between devices are 32-bit elements; how exact they have to be, the bound alone decides.
A program may use at most 128 MiB of HBM per device.

```python
import math
import jax
import jax.numpy as jnp
from jax import lax

H = 256
FE = 128
MID = 2
SAMP = 8
RAYS_GRP = 128
N_SLAB = 8
N_RAYS = 4


def draw_geometry(key, part):
    key_anchor = jax.random.fold_in(key, 11)
    key_angle = jax.random.fold_in(key, 12)
    key_height = jax.random.fold_in(key, 13)
    shape = (N_RAYS, RAYS_GRP)
    anchor = jax.random.uniform(key_anchor, (3,) + shape, jnp.float32, -1.0, 1.0)
    angle = jax.random.uniform(key_angle, shape, jnp.float32, -math.pi, math.pi)
    upright = jax.random.uniform(key_height, shape, jnp.float32, -1.0, 1.0)
    height = upright
    cycle = jnp.sqrt(jnp.maximum(1.0 - height * height, 0.0))
    direction = jnp.stack([cycle * jnp.cos(angle), cycle * jnp.sin(angle), height], axis=0)
    return jnp.concatenate([anchor, direction], axis=0).astype(jnp.float32)


def draw_freqs(key, part):
    shape = (N_SLAB, 3, FE)
    values = jnp.clip(1.5 * jax.random.normal(jax.random.fold_in(key, 22), shape, jnp.float32), -3.0, 3.0)
    return values.astype(jnp.float32)


def place_ends(entries, key, low, top_value):
    spot = [jax.random.randint(jax.random.fold_in(key, axis), (), 0, length) for axis, length in enumerate(entries.shape)]
    longest = entries.shape.index(max(entries.shape))
    next_to = spot[:longest] + [(spot[longest] + 1) % entries.shape[longest]] + spot[longest + 1:]
    return entries.at[tuple(spot)].set(low).at[tuple(next_to)].set(top_value)


def shard_levels(own_key, dims, split, least, largest):
    def one(position, blocks):
        draws = jax.random.uniform(jax.random.fold_in(jax.random.fold_in(own_key, 6), position), (blocks,), jnp.float32, least / len(split), largest / len(split))
        return jnp.repeat(jnp.exp(draws), dims[position] // blocks).reshape((-1,) + (1,) * (len(dims) - position - 1))

    factor_of = one(*split[0])
    for cut in split[1:]:
        factor_of = factor_of * one(*cut)
    return factor_of


def scatter_about(key, extent, deviation, most, pieces=(), kind=jnp.bfloat16):
    level = shard_levels(key, extent, pieces, -0.22, 0.18) if pieces else 1.0
    values = jax.random.normal(key, extent, jnp.float32) * deviation * level
    return jnp.minimum(jnp.maximum(values, -most), most).astype(kind)


def setup_inputs(seed: int = 0) -> dict:
    keys = jax.random.split(jax.random.key(seed), 11)
    return {
        "geometry": draw_geometry(jax.random.fold_in(keys[10], 71), 0),
        "entry": place_ends(jax.random.randint(keys[1], (N_SLAB, N_RAYS, RAYS_GRP), 0, SAMP * N_SLAB), jax.random.fold_in(keys[1], 1), 0, (SAMP * N_SLAB) - 1).astype(jnp.int32),
        "counts": place_ends(jax.random.randint(keys[2], (N_SLAB, N_RAYS, RAYS_GRP), 0, SAMP + 1), jax.random.fold_in(keys[2], 1), 0, SAMP).astype(jnp.int32),
        "targets": jnp.clip(1.0 * jax.random.uniform(keys[3], (3, N_RAYS, RAYS_GRP), jnp.float32) ** shard_levels(keys[3], (3, N_RAYS, RAYS_GRP), ((1, 4), (2, 8)), -0.2, 0.2), 0.0, 1.0),
        "w_in": scatter_about(keys[4], (N_SLAB, 2 * FE, H), (2 * FE) ** -0.5, 0.375, ((0, 8),), jnp.float32),
        "w_mid": scatter_about(keys[5], (N_SLAB, MID, H, H), H ** -0.5, 0.375, ((0, 8),), jnp.float32),
        "w_out": scatter_about(keys[6], (N_SLAB, 4, H), H ** -0.5, 0.375, ((0, 8),), jnp.float32),
        "b_hid": scatter_about(keys[7], (N_SLAB, MID + 1, H), 0.5, 3.0, ((0, 8),), jnp.float32),
        "b_out": scatter_about(keys[8], (N_SLAB, 4), 0.5, 3.0, ((0, 8),), jnp.float32),
        "freqs": draw_freqs(jax.random.fold_in(keys[10], 71), 0),
    }


HIGH = lax.Precision.HIGHEST

def segment(w_in, w_mid, w_out, b_hid, b_out, freqs, geometry, entry, counts, delta):
    width = geometry.shape[1]
    slots = jnp.arange(SAMP, dtype=jnp.int32)[:, None]
    times = 0.25 * (entry.astype(jnp.float32)[None, :] + slots.astype(jnp.float32) + 0.5)
    places = geometry[0:3, None, :] + times[None] * geometry[3:6, None, :]
    places = places.reshape(3, SAMP * width)
    phase = jnp.einsum('dk,dn->nk', freqs, places, precision=HIGH)
    hidden = jnp.concatenate([jnp.sin(phase), jnp.cos(phase)], axis=1)
    hidden = jax.nn.softplus(jnp.dot(hidden, w_in, precision=HIGH) + b_hid[0])
    for layer in range(MID):
        hidden = jax.nn.softplus(jnp.dot(hidden, w_mid[layer], precision=HIGH) + b_hid[layer + 1])
    result = jnp.einsum('ch,nh->cn', w_out, hidden, precision=HIGH) + b_out[:, None]
    sigma = jax.nn.softplus(result[0]).reshape(SAMP, width)
    colors = jax.nn.sigmoid(result[1:]).reshape(3, SAMP, width)
    alive = slots < counts[None, :]
    depth = jnp.where(alive, sigma * delta, jnp.float32(0.0))
    before = jnp.cumsum(depth, axis=0) - depth
    weights = jnp.exp(-before) * (1.0 - jnp.exp(-depth))
    color = lax.optimization_barrier(jnp.sum(weights[None] * colors, axis=1))
    logtrans = -lax.optimization_barrier(jnp.sum(depth, axis=0))
    return jnp.concatenate([color, logtrans[None]], axis=0)

def composite(segments, targets, factor):
    logtrans = segments[3]
    before = jnp.cumsum(logtrans, axis=0) - logtrans
    shade = jnp.exp(before)
    pixels = lax.optimization_barrier(jnp.sum(shade[None] * segments[:3], axis=1)) + jnp.exp(lax.optimization_barrier(jnp.sum(logtrans, axis=0)))[None]
    loss = factor * jnp.sum((pixels - targets) ** 2)
    return (loss, pixels)

def reference(geometry, entry, counts, targets, w_in, w_mid, w_out, b_hid, b_out, freqs):
    total = N_RAYS * RAYS_GRP
    delta = 3.0 / (SAMP * N_SLAB)
    factor = 1.0 / math.sqrt(3.0 * total)
    flat_geometry = geometry.reshape(6, total)
    flat_targets = targets.reshape(3, total)

    def forward(index):
        return segment(w_in[index], w_mid[index], w_out[index], b_hid[index], b_out[index], freqs[index], flat_geometry, entry[index].reshape(total), counts[index].reshape(total), delta)
    segments = lax.map(forward, jnp.arange(N_SLAB, dtype=jnp.int32))
    segments = jnp.transpose(segments, (1, 0, 2))
    loss, pullback, pixels = jax.vjp(lambda s: composite(s, flat_targets, factor), segments, has_aux=True)
    adjoint = pullback(jnp.ones((), jnp.float32))[0]

    def backward(index):

        def local(params):
            return segment(params[0], params[1], params[2], params[3], params[4], freqs[index], flat_geometry, entry[index].reshape(total), counts[index].reshape(total), delta)
        params = (w_in[index], w_mid[index], w_out[index], b_hid[index], b_out[index])
        unused, pull = jax.vjp(local, params)
        return pull(adjoint[:, index, :])[0]
    grads = lax.map(backward, jnp.arange(N_SLAB, dtype=jnp.int32))
    return (pixels.reshape(3, N_RAYS, RAYS_GRP), grads[0], grads[1], grads[2], grads[3], grads[4])
```

```python
import functools
import math

import jax
import jax.numpy as jnp
from jax import lax
from jax.experimental import pallas as pl
from jax.experimental.pallas import tpu as pltpu
from jax.sharding import PartitionSpec as P

SAMP = 8
F32 = jnp.float32
BF16 = jnp.bfloat16
MESH = pl.DeviceIdType.MESH
NT = (((1,), (1,)), ((), ()))


def split(x):
    hi = x.astype(BF16)
    return hi, (x - hi.astype(F32)).astype(BF16)


def mm(a, b):
    return jnp.dot(a, b, preferred_element_type=F32)


def mm_nt(a, b):
    return lax.dot_general(a, b, NT, preferred_element_type=F32)


def softplus(z):
    return jnp.maximum(z, 0.0) + jnp.log1p(jnp.exp(-jnp.abs(z)))


def sincos(x):
    k = jnp.round(x * F32(2.0 / math.pi))
    r = ((x - k * F32(1.5703125)) - k * F32(4.837512969970703e-4)) - k * F32(7.549789954891882e-8)
    q = k.astype(jnp.int32)
    r2 = r * r
    s = r + r * r2 * (F32(-1.6666654611e-1) + r2 * (F32(8.3321608736e-3) + r2 * F32(-1.9515295891e-4)))
    c = F32(1.0) - F32(0.5) * r2 + r2 * r2 * (
        F32(4.166664568298827e-2) + r2 * (F32(-1.388731625493765e-3) + r2 * F32(2.443315711809948e-5))
    )
    odd = (q & 1) == 1
    sn = jnp.where(odd, c, s)
    cs = jnp.where(odd, s, c)
    sn = jnp.where((q & 2) == 2, -sn, sn)
    cs = jnp.where(((q + 1) & 2) == 2, -cs, cs)
    return sn, cs


def kernel(
    slabs, n_rays, delta, factor,
    geo_ref, ent_ref, cnt_ref, tgt_ref, win_ref, wmid_ref, wout_ref, bhid_ref, bout_ref, fr_ref,
    pix_ref, gin_ref, gmid_ref, gout_ref, ghid_ref, gbout_ref,
    hh, hl, sg, dh, dl, wt, wn, seg_all, g, recv_a, recv_b, part, fin,
    seg_send, seg_recv, a_send, a_recv, b_send, b_recv, c_send, c_recv,
):
    me = lax.axis_index("slab")
    ray = lax.axis_index("rays")
    core = lax.rem(ray, 2)
    width = geo_ref.shape[2]
    own = tgt_ref.shape[2]
    n = SAMP * width
    hid = win_ref.shape[2]
    fe = fr_ref.shape[2]
    mid = wmid_ref.shape[1]
    layers = mid + 1
    bits = [b for b in range(1, 16) if (1 << b) < n_rays]
    chunk = 256
    n_chunks = n // chunk

    barrier = pltpu.get_barrier_semaphore()
    for k in range(1, slabs):
        pl.semaphore_signal(barrier, inc=1, device_id=(lax.rem(me + k, slabs), ray), device_id_type=MESH)
    peers = [1] + [1 << b for b in bits]

    def other(bit):
        place = lax.rem(ray // bit, 2)
        return ray + bit * (1 - 2 * place)

    for bit in peers:
        pl.semaphore_signal(barrier, inc=1, device_id=(me, other(bit)), device_id_type=MESH)

    def chunks(body):
        if n_chunks <= 4:
            for i in range(n_chunks):
                body(i * chunk)
        else:
            def step(i, carry):
                body(pl.multiple_of(i * chunk, chunk))
                return carry
            lax.fori_loop(0, n_chunks, step, 0)

    for l in range(layers):
        w = win_ref[0] if l == 0 else wmid_ref[0, l - 1]
        hi, lo = split(w.T)
        wt[l, 0] = hi
        wt[l, 1] = lo
        if l > 0:
            hi, lo = split(w)
            wn[l - 1, 0] = hi
            wn[l - 1, 1] = lo

    pad5 = jnp.zeros((8 - layers, hid), F32)
    bias = jnp.concatenate([bhid_ref[0], pad5], axis=0).T
    freq = jnp.concatenate([fr_ref[0], jnp.zeros((5, fe), F32)], axis=0).T

    geo = geo_ref[:, 0, :]
    t0 = 0.25 * (ent_ref[0].astype(F32) + 0.5)
    base = jnp.zeros((fe, width), F32)
    turn = jnp.zeros((fe, width), F32)
    for d in range(3):
        dirs = geo[3 + d:4 + d, :]
        place = geo[d:d + 1, :] + t0 * dirs
        base = base + freq[:, d:d + 1] * place
        turn = turn + freq[:, d:d + 1] * (0.25 * dirs)
    sn, cs = sincos(base)
    sd, cd = sincos(turn)
    for j in range(SAMP):
        lanes = slice(j * width, (j + 1) * width)
        hi, lo = split(sn)
        hh[0, 0:fe, lanes] = hi
        hl[0, 0:fe, lanes] = lo
        hi, lo = split(cs)
        hh[0, fe:2 * fe, lanes] = hi
        hl[0, fe:2 * fe, lanes] = lo
        if j < SAMP - 1:
            sn, cs = sn * cd + cs * sd, cs * cd - sn * sd

    for l in range(layers):
        def layer(at, l=l):
            lanes = pl.ds(at, chunk)
            hi = hh[l, :, lanes]
            z = mm(wt[l, 0], hi) + mm(wt[l, 1], hi) + mm(wt[l, 0], hl[l, :, lanes])
            z = z + bias[:, l:l + 1]
            h = softplus(z)
            sg[l, :, lanes] = jnp.exp(z - h)
            hi, lo = split(h)
            hh[l + 1, :, lanes] = hi
            hl[l + 1, :, lanes] = lo
        chunks(layer)

    wo = jnp.concatenate([wout_ref[0], jnp.zeros((4, hid), F32)], axis=0)
    wo_hi, wo_lo = split(wo)
    last_hi = hh[layers]
    out = mm(wo_hi, last_hi) + mm(wo_lo, last_hi) + mm(wo_hi, hl[layers])
    bout = jnp.concatenate([bout_ref[...], jnp.zeros((7, 4), F32)], axis=0)
    counts = cnt_ref[0]
    sigma = softplus(out[0:1] + bout[0:1, 0:1])
    sigma_slope = jnp.exp(out[0:1] + bout[0:1, 0:1] - sigma)
    rgb = []
    for c in range(3):
        o = out[c + 1:c + 2] + bout[0:1, c + 1:c + 2]
        rgb.append(jnp.exp(o - softplus(o)))
    rgb = jnp.concatenate(rgb, axis=0)
    before = jnp.zeros((1, width), F32)
    color = jnp.zeros((3, width), F32)
    weight, after, live, tints = [], [], [], []
    for j in range(SAMP):
        lanes = slice(j * width, (j + 1) * width)
        alive = counts > j
        tau = jnp.where(alive, sigma[:, lanes] * delta, 0.0)
        e0 = jnp.exp(-before)
        e1 = jnp.exp(-tau)
        w = e0 * (1.0 - e1)
        tint = rgb[:, lanes]
        color = color + w * tint
        before = before + tau
        weight.append(w)
        after.append(e0 * e1)
        live.append(alive)
        tints.append(tint)
    mine = lax.broadcasted_iota(jnp.int32, (own, width), 1) == (
        lax.broadcasted_iota(jnp.int32, (own, width), 0) + me * own
    )
    spread = jnp.where(mine, 1.0, 0.0).astype(F32)
    spot = jnp.dot(tgt_ref[:, 0, :], spread, precision=lax.Precision.HIGHEST, preferred_element_type=F32)
    seg_all[me] = jnp.concatenate([color, -before, spot, jnp.zeros((1, width), F32)], axis=0)

    pl.semaphore_wait(barrier, slabs - 1 + len(peers))
    copies = []
    for k in range(1, slabs):
        copy = pltpu.make_async_remote_copy(
            src_ref=seg_all.at[me], dst_ref=seg_all.at[me],
            send_sem=seg_send.at[k], recv_sem=seg_recv.at[k],
            device_id=(lax.rem(me + k, slabs), ray), device_id_type=MESH,
        )
        copy.start()
        copies.append(copy)
    for copy in copies:
        copy.wait()

    total = jnp.zeros((1, width), F32)
    pixels = jnp.zeros((3, width), F32)
    target = jnp.zeros((3, width), F32)
    shades, colors = [], []
    mine_shade = jnp.zeros((1, width), F32)
    for s in range(slabs):
        block = seg_all[s]
        shade = jnp.exp(total)
        pixels = pixels + shade * block[0:3]
        target = target + block[4:7]
        total = total + block[3:4]
        mine_shade = mine_shade + jnp.where(me == s, shade, 0.0)
        shades.append(shade)
        colors.append(block[0:3])
    clear = jnp.exp(total)
    pixels = pixels + clear
    pull = (2.0 * factor) * (pixels - target)
    d_log = clear * jnp.sum(pull, axis=0, keepdims=True)
    for s in range(slabs):
        term = shades[s] * jnp.sum(pull * colors[s], axis=0, keepdims=True)
        d_log = d_log + jnp.where(me < s, term, 0.0)
    d_color = mine_shade * pull
    pix_ref[:, 0, :] = lax.dot_general(
        pixels, spread, NT, precision=lax.Precision.HIGHEST, preferred_element_type=F32
    )

    later = jnp.zeros((1, width), F32)
    d_out = [None] * SAMP
    for j in reversed(range(SAMP)):
        lanes = slice(j * width, (j + 1) * width)
        u = jnp.sum(d_color * tints[j], axis=0, keepdims=True)
        d_tau = after[j] * u - later - d_log
        later = later + weight[j] * u
        d0 = jnp.where(live[j], d_tau * delta * sigma_slope[:, lanes], 0.0)
        d_rgb = d_color * weight[j] * tints[j] * (1.0 - tints[j])
        d_out[j] = jnp.concatenate([d0, d_rgb, jnp.zeros((4, width), F32)], axis=0)
    d_out = jnp.concatenate(d_out, axis=1)
    do_hi, do_lo = split(d_out)
    wot_hi, wot_lo = split(wo.T)

    def last(at):
        lanes = pl.ds(at, chunk)
        hi, lo = (d_hi_ref(at), d_lo_ref(at))
        d = mm(wot_hi, hi) + mm(wot_lo, hi) + mm(wot_hi, lo)
        hi, lo = split(d * sg[layers - 1, :, lanes])
        dh[0, :, lanes] = hi
        dl[0, :, lanes] = lo

    dh[1, 0:8, :] = do_hi
    dl[1, 0:8, :] = do_lo

    def d_hi_ref(at):
        return dh[1, 0:8, pl.ds(at, chunk)]

    def d_lo_ref(at):
        return dl[1, 0:8, pl.ds(at, chunk)]

    small = hid
    ones = jnp.ones((16, n), BF16)
    g[layers - 1, small:small + 16, :] = jnp.zeros((16, hid), F32)
    g_out = mm_nt(do_hi, last_hi) + mm_nt(do_lo, last_hi) + mm_nt(do_hi, hl[layers])
    g[layers - 1, small:small + 4, :] = g_out[0:4]
    row = mm_nt(ones, do_hi) + mm_nt(ones, do_lo)
    g[layers - 1, small + 7:small + 8, 0:8] = row[0:1, 0:8]
    chunks(last)

    def rows_of(b):
        return hid + 16 if b == layers - 1 else hid

    def stage_a(b):
        half = rows_of(b) // 2
        return pltpu.make_async_remote_copy(
            src_ref=g.at[b, pl.ds(pl.multiple_of((1 - core) * half, 8), half)],
            dst_ref=recv_a.at[b, pl.ds(0, half)],
            send_sem=a_send.at[b], recv_sem=a_recv.at[b],
            device_id=(me, other(1)), device_id_type=MESH,
        )

    def stage_b(b, i):
        half = rows_of(b) // 2
        return pltpu.make_async_remote_copy(
            src_ref=part.at[b, i, pl.ds(0, half)], dst_ref=recv_b.at[b, i, pl.ds(0, half)],
            send_sem=b_send.at[b, i], recv_sem=b_recv.at[b, i],
            device_id=(me, other(1 << bits[i])), device_id_type=MESH,
        )

    def stage_c(b):
        half = rows_of(b) // 2
        rows = pl.ds(pl.multiple_of(core * half, 8), half)
        return pltpu.make_async_remote_copy(
            src_ref=fin.at[b, rows], dst_ref=fin.at[b, rows],
            send_sem=c_send.at[b], recv_sem=c_recv.at[b],
            device_id=(me, other(1)), device_id_type=MESH,
        )

    def after_a(b):
        half = rows_of(b) // 2
        stage_a(b).wait()
        value = g[b, pl.ds(pl.multiple_of(core * half, 8), half), :] + recv_a[b, 0:half, :]
        if bits:
            part[b, 0, 0:half, :] = value
            stage_b(b, 0).start()
        else:
            fin[b, pl.ds(pl.multiple_of(core * half, 8), half), :] = value
            stage_c(b).start()

    def after_b(b, i):
        half = rows_of(b) // 2
        stage_b(b, i).wait()
        value = part[b, i, 0:half, :] + recv_b[b, i, 0:half, :]
        if i + 1 < len(bits):
            part[b, i + 1, 0:half, :] = value
            stage_b(b, i + 1).start()
        else:
            fin[b, pl.ds(pl.multiple_of(core * half, 8), half), :] = value
            stage_c(b).start()

    steps = []
    for b in range(layers):
        steps.append([functools.partial(after_a, b)] + [functools.partial(after_b, b, i) for i in range(len(bits))])

    for b in range(layers):
        l = layers - 1 - b
        slot = b % 2
        dz_hi, dz_lo = dh[slot], dl[slot]
        lh = hh[l]
        grad = mm_nt(lh, dz_hi) + mm_nt(lh, dz_lo) + mm_nt(hl[l], dz_hi)
        bias_row = mm_nt(ones, dz_hi) + mm_nt(ones, dz_lo)
        g[b, 0:hid, :] = grad
        g[layers - 1, small + 4 + l:small + 5 + l, :] = bias_row[0:1]
        stage_a(b).start()
        for earlier in range(b):
            if steps[earlier]:
                steps[earlier].pop(0)()
        if l > 0:
            def back(at, l=l, slot=slot):
                lanes = pl.ds(at, chunk)
                hi = dh[slot, :, lanes]
                d = mm(wn[l - 1, 0], hi) + mm(wn[l - 1, 1], hi) + mm(wn[l - 1, 0], dl[slot, :, lanes])
                hi, lo = split(d * sg[l - 1, :, lanes])
                dh[1 - slot, :, lanes] = hi
                dl[1 - slot, :, lanes] = lo
            chunks(back)
            if steps[b]:
                steps[b].pop(0)()
    while any(steps):
        for b in range(layers):
            if steps[b]:
                steps[b].pop(0)()
    for b in range(layers):
        stage_c(b).wait()
        l = layers - 1 - b
        if l > 0:
            gmid_ref[0, l - 1] = fin[b, 0:hid, :]
        else:
            gin_ref[0] = fin[b, 0:hid, :]
    tail = fin[layers - 1, small:small + 16, :]
    gout_ref[0] = tail[0:4]
    ghid_ref[0] = tail[4:4 + layers]
    gbout_ref[...] = tail[7:8, 0:4]


def solution(mesh):
    slabs, n_rays = mesh.shape["slab"], mesh.shape["rays"]

    def shards(geometry, entry, counts, targets, w_in, w_mid, w_out, b_hid, b_out, freqs):
        width = geometry.shape[2]
        own = targets.shape[2]
        n = SAMP * width
        hid = w_in.shape[2]
        mid = w_mid.shape[1]
        layers = mid + 1
        delta = 3.0 / (SAMP * slabs)
        factor = 1.0 / math.sqrt(3.0 * n_rays * slabs * own)
        more = max(1, sum(1 for b in range(1, 16) if (1 << b) < n_rays))
        half = (hid + 16) // 2
        shape = jax.ShapeDtypeStruct
        return pl.pallas_call(
            functools.partial(kernel, slabs, n_rays, delta, factor),
            out_shape=(
                shape((3, 1, own), F32),
                shape((1, 2 * freqs.shape[2], hid), F32),
                shape((1, mid, hid, hid), F32),
                shape((1, 4, hid), F32),
                shape((1, layers, hid), F32),
                shape((1, 4), F32),
            ),
            in_specs=[pl.BlockSpec(memory_space=pltpu.VMEM)] * 10,
            out_specs=tuple([pl.BlockSpec(memory_space=pltpu.VMEM)] * 6),
            scratch_shapes=[
                pltpu.VMEM((layers + 1, hid, n), BF16),
                pltpu.VMEM((layers + 1, hid, n), BF16),
                pltpu.VMEM((layers, hid, n), F32),
                pltpu.VMEM((2, hid, n), BF16),
                pltpu.VMEM((2, hid, n), BF16),
                pltpu.VMEM((layers, 2, hid, hid), BF16),
                pltpu.VMEM((mid, 2, hid, hid), BF16),
                pltpu.VMEM((slabs, 8, width), F32),
                pltpu.VMEM((layers, hid + 16, hid), F32),
                pltpu.VMEM((layers, half, hid), F32),
                pltpu.VMEM((layers, more, half, hid), F32),
                pltpu.VMEM((layers, more, half, hid), F32),
                pltpu.VMEM((layers, hid + 16, hid), F32),
                pltpu.SemaphoreType.DMA((slabs,)),
                pltpu.SemaphoreType.DMA((slabs,)),
                pltpu.SemaphoreType.DMA((layers,)),
                pltpu.SemaphoreType.DMA((layers,)),
                pltpu.SemaphoreType.DMA((layers, more)),
                pltpu.SemaphoreType.DMA((layers, more)),
                pltpu.SemaphoreType.DMA((layers,)),
                pltpu.SemaphoreType.DMA((layers,)),
            ],
            compiler_params=pltpu.CompilerParams(
                collective_id=0, has_side_effects=True, vmem_limit_bytes=60 * 1024 * 1024
            ),
        )(geometry, entry, counts, targets, w_in, w_mid, w_out, b_hid, b_out, freqs)

    in_specs = (
        P(None, "rays", None),
        P("slab", "rays", None),
        P("slab", "rays", None),
        P(None, "rays", "slab"),
        P("slab", None, None),
        P("slab", None, None, None),
        P("slab", None, None),
        P("slab", None, None),
        P("slab", None),
        P("slab", None, None),
    )
    out_specs = (
        P(None, "rays", "slab"),
        P("slab", None, None),
        P("slab", None, None, None),
        P("slab", None, None),
        P("slab", None, None),
        P("slab", None),
    )
    return jax.shard_map(shards, mesh=mesh, in_specs=in_specs, out_specs=out_specs, check_vma=False)
```

```python
import functools
import math

import jax
import jax.numpy as jnp
from jax import lax
from jax.experimental import pallas as pl
from jax.experimental.pallas import tpu as pltpu
from jax.sharding import PartitionSpec as P

SAMP = 8
F32 = jnp.float32
BF16 = jnp.bfloat16
MESH = pl.DeviceIdType.MESH
NT = (((1,), (1,)), ((), ()))


def split(x):
    hi = x.astype(BF16)
    return hi, (x - hi.astype(F32)).astype(BF16)


def mm(a, b):
    return jnp.dot(a, b, preferred_element_type=F32)


def mm_nt(a, b):
    return lax.dot_general(a, b, NT, preferred_element_type=F32)


def softplus(z):
    return jnp.maximum(z, 0.0) + jnp.log1p(jnp.exp(-jnp.abs(z)))


def sincos(x):
    k = jnp.round(x * F32(2.0 / math.pi))
    r = ((x - k * F32(1.5703125)) - k * F32(4.837512969970703e-4)) - k * F32(7.549789954891882e-8)
    q = k.astype(jnp.int32)
    r2 = r * r
    s = r + r * r2 * (F32(-1.6666654611e-1) + r2 * (F32(8.3321608736e-3) + r2 * F32(-1.9515295891e-4)))
    c = F32(1.0) - F32(0.5) * r2 + r2 * r2 * (
        F32(4.166664568298827e-2) + r2 * (F32(-1.388731625493765e-3) + r2 * F32(2.443315711809948e-5))
    )
    odd = (q & 1) == 1
    sn = jnp.where(odd, c, s)
    cs = jnp.where(odd, s, c)
    sn = jnp.where((q & 2) == 2, -sn, sn)
    cs = jnp.where(((q + 1) & 2) == 2, -cs, cs)
    return sn, cs


def kernel(
    slabs, n_rays, delta, factor,
    *refs,
):
    far, (pix_ref, fin), near = refs[:10], refs[10:12], refs[12:22]
    geo_ref, ent_ref, cnt_ref, tgt_ref, win_ref, wmid_ref, wout_ref, bhid_ref, bout_ref, fr_ref = near
    hh, hl, sg, dh, dl, wt, wn, seg_all, g, recv_a, recv_b, part = refs[22:34]
    load_sem, seg_send, seg_recv, a_send, a_recv, b_send, b_recv, c_send, c_recv = refs[34:]
    loads = [pltpu.make_async_copy(far[i], near[i], load_sem.at[i]) for i in range(10)]
    for i in (0, 1, 9, 4, 7, 5, 6, 8, 2, 3):
        loads[i].start()
    me = lax.axis_index("slab")
    ray = lax.axis_index("rays")
    core = lax.rem(ray, 2)
    width = geo_ref.shape[2]
    own = tgt_ref.shape[2]
    n = SAMP * width
    hid = win_ref.shape[2]
    fe = fr_ref.shape[2]
    mid = wmid_ref.shape[1]
    layers = mid + 1
    bits = [b for b in range(1, 16) if (1 << b) < n_rays]
    chunk = 256
    n_chunks = n // chunk

    barrier = pltpu.get_barrier_semaphore()
    for k in range(1, slabs):
        pl.semaphore_signal(barrier, inc=1, device_id=(lax.rem(me + k, slabs), ray), device_id_type=MESH)
    peers = [1] + [1 << b for b in bits]

    def other(bit):
        place = lax.rem(ray // bit, 2)
        return ray + bit * (1 - 2 * place)

    for bit in peers:
        pl.semaphore_signal(barrier, inc=1, device_id=(me, other(bit)), device_id_type=MESH)

    def chunks(body):
        if n_chunks <= 4:
            for i in range(n_chunks):
                body(i * chunk)
        else:
            def step(i, carry):
                body(pl.multiple_of(i * chunk, chunk))
                return carry
            lax.fori_loop(0, n_chunks, step, 0)

    for i in (0, 1, 9):
        loads[i].wait()
    freq = jnp.concatenate([fr_ref[:, 0, :], jnp.zeros((5, fe), F32)], axis=0).T

    geo = geo_ref[:, 0, :]
    t0 = 0.25 * (ent_ref[0].astype(F32) + 0.5)
    base = jnp.zeros((fe, width), F32)
    turn = jnp.zeros((fe, width), F32)
    for d in range(3):
        dirs = geo[3 + d:4 + d, :]
        place = geo[d:d + 1, :] + t0 * dirs
        base = base + freq[:, d:d + 1] * place
        turn = turn + freq[:, d:d + 1] * (0.25 * dirs)
    sn, cs = sincos(base)
    sd, cd = sincos(turn)
    for j in range(SAMP):
        lanes = slice(j * width, (j + 1) * width)
        hi, lo = split(sn)
        hh[0, 0:fe, lanes] = hi
        hl[0, 0:fe, lanes] = lo
        hi, lo = split(cs)
        hh[0, fe:2 * fe, lanes] = hi
        hl[0, fe:2 * fe, lanes] = lo
        if j < SAMP - 1:
            sn, cs = sn * cd + cs * sd, cs * cd - sn * sd

    for i in (2, 3, 4, 5, 6, 7, 8):
        loads[i].wait()
    for l in range(layers):
        w = win_ref[0] if l == 0 else wmid_ref[0, l - 1]
        hi, lo = split(w.T)
        wt[l, 0] = hi
        wt[l, 1] = lo
        if l > 0:
            hi, lo = split(w)
            wn[l - 1, 0] = hi
            wn[l - 1, 1] = lo

    pad5 = jnp.zeros((8 - layers, hid), F32)
    bias = jnp.concatenate([bhid_ref[:, 0, :], pad5], axis=0).T

    for l in range(layers):
        def layer(at, l=l):
            lanes = pl.ds(at, chunk)
            hi = hh[l, :, lanes]
            z = mm(wt[l, 0], hi) + mm(wt[l, 1], hi) + mm(wt[l, 0], hl[l, :, lanes])
            z = z + bias[:, l:l + 1]
            h = softplus(z)
            sg[l, :, lanes] = jnp.exp(z - h)
            hi, lo = split(h)
            hh[l + 1, :, lanes] = hi
            hl[l + 1, :, lanes] = lo
        chunks(layer)

    wo = jnp.concatenate([wout_ref[0], jnp.zeros((4, hid), F32)], axis=0)
    wo_hi, wo_lo = split(wo)
    last_hi = hh[layers]
    out = mm(wo_hi, last_hi) + mm(wo_lo, last_hi) + mm(wo_hi, hl[layers])
    bout = jnp.concatenate([bout_ref[...], jnp.zeros((7, 4), F32)], axis=0)
    counts = cnt_ref[0]
    sigma = softplus(out[0:1] + bout[0:1, 0:1])
    sigma_slope = jnp.exp(out[0:1] + bout[0:1, 0:1] - sigma)
    rgb = []
    for c in range(3):
        o = out[c + 1:c + 2] + bout[0:1, c + 1:c + 2]
        rgb.append(jnp.exp(o - softplus(o)))
    rgb = jnp.concatenate(rgb, axis=0)
    before = jnp.zeros((1, width), F32)
    color = jnp.zeros((3, width), F32)
    weight, after, live, tints = [], [], [], []
    for j in range(SAMP):
        lanes = slice(j * width, (j + 1) * width)
        alive = counts > j
        tau = jnp.where(alive, sigma[:, lanes] * delta, 0.0)
        e0 = jnp.exp(-before)
        e1 = jnp.exp(-tau)
        w = e0 * (1.0 - e1)
        tint = rgb[:, lanes]
        color = color + w * tint
        before = before + tau
        weight.append(w)
        after.append(e0 * e1)
        live.append(alive)
        tints.append(tint)
    mine = lax.broadcasted_iota(jnp.int32, (own, width), 1) == (
        lax.broadcasted_iota(jnp.int32, (own, width), 0) + me * own
    )
    spread = jnp.where(mine, 1.0, 0.0).astype(F32)
    spot = jnp.dot(tgt_ref[:, 0, :], spread, precision=lax.Precision.HIGHEST, preferred_element_type=F32)
    seg_all[me] = jnp.concatenate([color, -before, spot, jnp.zeros((1, width), F32)], axis=0)

    pl.semaphore_wait(barrier, slabs - 1 + len(peers))
    copies = []
    for k in range(1, slabs):
        copy = pltpu.make_async_remote_copy(
            src_ref=seg_all.at[me], dst_ref=seg_all.at[me],
            send_sem=seg_send.at[k], recv_sem=seg_recv.at[k],
            device_id=(lax.rem(me + k, slabs), ray), device_id_type=MESH,
        )
        copy.start()
        copies.append(copy)
    for copy in copies:
        copy.wait()

    total = jnp.zeros((1, width), F32)
    pixels = jnp.zeros((3, width), F32)
    target = jnp.zeros((3, width), F32)
    shades, colors = [], []
    mine_shade = jnp.zeros((1, width), F32)
    for s in range(slabs):
        block = seg_all[s]
        shade = jnp.exp(total)
        pixels = pixels + shade * block[0:3]
        target = target + block[4:7]
        total = total + block[3:4]
        mine_shade = mine_shade + jnp.where(me == s, shade, 0.0)
        shades.append(shade)
        colors.append(block[0:3])
    clear = jnp.exp(total)
    pixels = pixels + clear
    pull = (2.0 * factor) * (pixels - target)
    d_log = clear * jnp.sum(pull, axis=0, keepdims=True)
    for s in range(slabs):
        term = shades[s] * jnp.sum(pull * colors[s], axis=0, keepdims=True)
        d_log = d_log + jnp.where(me < s, term, 0.0)
    d_color = mine_shade * pull
    pix_ref[...] = lax.dot_general(
        pixels, spread, NT, precision=lax.Precision.HIGHEST, preferred_element_type=F32
    )

    later = jnp.zeros((1, width), F32)
    d_out = [None] * SAMP
    for j in reversed(range(SAMP)):
        lanes = slice(j * width, (j + 1) * width)
        u = jnp.sum(d_color * tints[j], axis=0, keepdims=True)
        d_tau = after[j] * u - later - d_log
        later = later + weight[j] * u
        d0 = jnp.where(live[j], d_tau * delta * sigma_slope[:, lanes], 0.0)
        d_rgb = d_color * weight[j] * tints[j] * (1.0 - tints[j])
        d_out[j] = jnp.concatenate([d0, d_rgb, jnp.zeros((4, width), F32)], axis=0)
    d_out = jnp.concatenate(d_out, axis=1)
    do_hi, do_lo = split(d_out)
    wot_hi, wot_lo = split(wo.T)

    def last(at):
        lanes = pl.ds(at, chunk)
        hi, lo = (d_hi_ref(at), d_lo_ref(at))
        d = mm(wot_hi, hi) + mm(wot_lo, hi) + mm(wot_hi, lo)
        hi, lo = split(d * sg[layers - 1, :, lanes])
        dh[0, :, lanes] = hi
        dl[0, :, lanes] = lo

    dh[1, 0:8, :] = do_hi
    dl[1, 0:8, :] = do_lo

    def d_hi_ref(at):
        return dh[1, 0:8, pl.ds(at, chunk)]

    def d_lo_ref(at):
        return dl[1, 0:8, pl.ds(at, chunk)]

    small = hid
    ones = jnp.ones((16, n), BF16)
    g[layers - 1, small:small + 16, :] = jnp.zeros((16, hid), F32)
    g_out = mm_nt(do_hi, last_hi) + mm_nt(do_lo, last_hi) + mm_nt(do_hi, hl[layers])
    g[layers - 1, small:small + 4, :] = g_out[0:4]
    row = mm_nt(ones, do_hi) + mm_nt(ones, do_lo)
    g[layers - 1, small + 7:small + 8, 0:8] = row[0:1, 0:8]
    chunks(last)

    def rows_of(b):
        return hid + 16 if b == layers - 1 else hid

    def stage_a(b):
        half = rows_of(b) // 2
        return pltpu.make_async_remote_copy(
            src_ref=g.at[b, pl.ds(pl.multiple_of((1 - core) * half, 8), half)],
            dst_ref=recv_a.at[b, pl.ds(0, half)],
            send_sem=a_send.at[b], recv_sem=a_recv.at[b],
            device_id=(me, other(1)), device_id_type=MESH,
        )

    def stage_b(b, i):
        half = rows_of(b) // 2
        return pltpu.make_async_remote_copy(
            src_ref=part.at[b, i, pl.ds(0, half)], dst_ref=recv_b.at[b, i, pl.ds(0, half)],
            send_sem=b_send.at[b, i], recv_sem=b_recv.at[b, i],
            device_id=(me, other(1 << bits[i])), device_id_type=MESH,
        )

    def stage_c(b):
        half = rows_of(b) // 2
        rows = pl.ds(pl.multiple_of(core * half, 8), half)
        return pltpu.make_async_remote_copy(
            src_ref=fin.at[b, rows], dst_ref=fin.at[b, rows],
            send_sem=c_send.at[b], recv_sem=c_recv.at[b],
            device_id=(me, other(1)), device_id_type=MESH,
        )

    def after_a(b):
        half = rows_of(b) // 2
        stage_a(b).wait()
        value = g[b, pl.ds(pl.multiple_of(core * half, 8), half), :] + recv_a[b, 0:half, :]
        if bits:
            part[b, 0, 0:half, :] = value
            stage_b(b, 0).start()
        else:
            fin[b, pl.ds(pl.multiple_of(core * half, 8), half), :] = value
            stage_c(b).start()

    def after_b(b, i):
        half = rows_of(b) // 2
        stage_b(b, i).wait()
        value = part[b, i, 0:half, :] + recv_b[b, i, 0:half, :]
        if i + 1 < len(bits):
            part[b, i + 1, 0:half, :] = value
            stage_b(b, i + 1).start()
        else:
            fin[b, pl.ds(pl.multiple_of(core * half, 8), half), :] = value
            stage_c(b).start()

    steps = []
    for b in range(layers):
        steps.append([functools.partial(after_a, b)] + [functools.partial(after_b, b, i) for i in range(len(bits))])

    for b in range(layers):
        l = layers - 1 - b
        slot = b % 2
        dz_hi, dz_lo = dh[slot], dl[slot]
        lh = hh[l]
        grad = mm_nt(lh, dz_hi) + mm_nt(lh, dz_lo) + mm_nt(hl[l], dz_hi)
        bias_row = mm_nt(ones, dz_hi) + mm_nt(ones, dz_lo)
        g[b, 0:hid, :] = grad
        g[layers - 1, small + 4 + l:small + 5 + l, :] = bias_row[0:1]
        stage_a(b).start()
        for earlier in range(b):
            if steps[earlier]:
                steps[earlier].pop(0)()
        if l > 0:
            def back(at, l=l, slot=slot):
                lanes = pl.ds(at, chunk)
                hi = dh[slot, :, lanes]
                d = mm(wn[l - 1, 0], hi) + mm(wn[l - 1, 1], hi) + mm(wn[l - 1, 0], dl[slot, :, lanes])
                hi, lo = split(d * sg[l - 1, :, lanes])
                dh[1 - slot, :, lanes] = hi
                dl[1 - slot, :, lanes] = lo
            chunks(back)
            if steps[b]:
                steps[b].pop(0)()
    while any(steps):
        for b in range(layers):
            if steps[b]:
                steps[b].pop(0)()
    for b in range(layers):
        stage_c(b).wait()


def unpack(pix_in, fin, pix_ref, gin_ref, gmid_ref, gout_ref, ghid_ref, gbout_ref, sems):
    layers = fin.shape[0]
    hid = fin.shape[2]
    copies = []
    for l in range(layers):
        place = gin_ref.at[0] if l == 0 else gmid_ref.at[0, l - 1]
        copies.append(pltpu.make_async_copy(fin.at[layers - 1 - l, pl.ds(0, hid)], place, sems.at[l]))
    for copy in copies:
        copy.start()
    tail = fin[layers - 1, hid:hid + 16, :]
    gout_ref[0] = tail[0:4]
    ghid_ref[:, 0, :] = tail[4:4 + layers]
    gbout_ref[...] = tail[7:8, 0:4]
    pix_ref[:, 0, :] = pix_in[0:3, :]
    for copy in copies:
        copy.wait()


def solution(mesh):
    slabs, n_rays = mesh.shape["slab"], mesh.shape["rays"]

    def shards(geometry, entry, counts, targets, w_in, w_mid, w_out, b_hid, b_out, freqs):
        width = geometry.shape[2]
        own = targets.shape[2]
        n = SAMP * width
        hid = w_in.shape[2]
        mid = w_mid.shape[1]
        layers = mid + 1
        delta = 3.0 / (SAMP * slabs)
        factor = 1.0 / math.sqrt(3.0 * n_rays * slabs * own)
        more = max(1, sum(1 for b in range(1, 16) if (1 << b) < n_rays))
        half = (hid + 16) // 2
        shape = jax.ShapeDtypeStruct
        args = (
            geometry, entry, counts, targets, w_in, w_mid, w_out,
            jnp.transpose(b_hid, (1, 0, 2)), b_out, jnp.transpose(freqs, (1, 0, 2)),
        )
        vmem = pl.BlockSpec(memory_space=pltpu.VMEM)
        item = 4 * hid * n
        need = item * (2 * layers + 4) + item * layers + 16 * (1 << 20) + 64 * slabs * width
        pixels, packed = pl.pallas_call(
            functools.partial(kernel, slabs, n_rays, delta, factor),
            out_shape=(shape((3, own), F32), shape((layers, hid + 16, hid), F32)),
            in_specs=[pl.BlockSpec(memory_space=pltpu.HBM)] * 10,
            out_specs=(vmem, vmem),
            scratch_shapes=[pltpu.VMEM(a.shape, a.dtype) for a in args] + [
                pltpu.VMEM((layers + 1, hid, n), BF16),
                pltpu.VMEM((layers + 1, hid, n), BF16),
                pltpu.VMEM((layers, hid, n), F32),
                pltpu.VMEM((2, hid, n), BF16),
                pltpu.VMEM((2, hid, n), BF16),
                pltpu.VMEM((layers, 2, hid, hid), BF16),
                pltpu.VMEM((mid, 2, hid, hid), BF16),
                pltpu.VMEM((slabs, 8, width), F32),
                pltpu.VMEM((layers, hid + 16, hid), F32),
                pltpu.VMEM((layers, half, hid), F32),
                pltpu.VMEM((layers, more, half, hid), F32),
                pltpu.VMEM((layers, more, half, hid), F32),
                pltpu.SemaphoreType.DMA((10,)),
                pltpu.SemaphoreType.DMA((slabs,)),
                pltpu.SemaphoreType.DMA((slabs,)),
                pltpu.SemaphoreType.DMA((layers,)),
                pltpu.SemaphoreType.DMA((layers,)),
                pltpu.SemaphoreType.DMA((layers, more)),
                pltpu.SemaphoreType.DMA((layers, more)),
                pltpu.SemaphoreType.DMA((layers,)),
                pltpu.SemaphoreType.DMA((layers,)),
            ],
            compiler_params=pltpu.CompilerParams(
                collective_id=0, has_side_effects=True, vmem_limit_bytes=min(need, 60 << 20)
            ),
        )(*args)
        hbm = pl.BlockSpec(memory_space=pltpu.HBM)
        outs = pl.pallas_call(
            unpack,
            out_shape=(
                shape((3, 1, own), F32),
                shape((1, 2 * freqs.shape[2], hid), F32),
                shape((1, mid, hid, hid), F32),
                shape((1, 4, hid), F32),
                shape((layers, 1, hid), F32),
                shape((1, 4), F32),
            ),
            in_specs=[vmem] * 2,
            out_specs=(vmem, hbm, hbm, vmem, vmem, vmem),
            scratch_shapes=[pltpu.SemaphoreType.DMA((layers,))],
            compiler_params=pltpu.CompilerParams(vmem_limit_bytes=8 << 20),
        )(pixels, packed)
        return outs[:4] + (jnp.transpose(outs[4], (1, 0, 2)), outs[5])

    in_specs = (
        P(None, "rays", None),
        P("slab", "rays", None),
        P("slab", "rays", None),
        P(None, "rays", "slab"),
        P("slab", None, None),
        P("slab", None, None, None),
        P("slab", None, None),
        P("slab", None, None),
        P("slab", None),
        P("slab", None, None),
    )
    out_specs = (
        P(None, "rays", "slab"),
        P("slab", None, None),
        P("slab", None, None, None),
        P("slab", None, None),
        P("slab", None, None),
        P("slab", None),
    )
    return jax.shard_map(shards, mesh=mesh, in_specs=in_specs, out_specs=out_specs, check_vma=False)
```

```python
import functools
import math

import jax
import jax.numpy as jnp
from jax import lax
from jax.experimental import pallas as pl
from jax.experimental.pallas import tpu as pltpu
from jax.sharding import PartitionSpec as P

SAMP = 8
F32 = jnp.float32
BF16 = jnp.bfloat16
MESH = pl.DeviceIdType.MESH
NT = (((1,), (1,)), ((), ()))


def split(x):
    hi = x.astype(BF16)
    return hi, (x - hi.astype(F32)).astype(BF16)


def mm(a, b):
    return jnp.dot(a, b, preferred_element_type=F32)


def mm_nt(a, b):
    return lax.dot_general(a, b, NT, preferred_element_type=F32)


def softplus(z):
    return jnp.maximum(z, 0.0) + jnp.log1p(jnp.exp(-jnp.abs(z)))


def sincos(x):
    k = jnp.round(x * F32(2.0 / math.pi))
    r = ((x - k * F32(1.5703125)) - k * F32(4.837512969970703e-4)) - k * F32(7.549789954891882e-8)
    q = k.astype(jnp.int32)
    r2 = r * r
    s = r + r * r2 * (F32(-1.6666654611e-1) + r2 * (F32(8.3321608736e-3) + r2 * F32(-1.9515295891e-4)))
    c = F32(1.0) - F32(0.5) * r2 + r2 * r2 * (
        F32(4.166664568298827e-2) + r2 * (F32(-1.388731625493765e-3) + r2 * F32(2.443315711809948e-5))
    )
    odd = (q & 1) == 1
    sn = jnp.where(odd, c, s)
    cs = jnp.where(odd, s, c)
    sn = jnp.where((q & 2) == 2, -sn, sn)
    cs = jnp.where(((q + 1) & 2) == 2, -cs, cs)
    return sn, cs


def kernel(
    slabs, n_rays, delta, factor,
    *refs,
):
    far, (pix_ref, fin), near = refs[:10], refs[10:12], refs[12:22]
    geo_ref, ent_ref, cnt_ref, tgt_ref, win_ref, wmid_ref, wout_ref, bhid_ref, bout_ref, fr_ref = near
    hx, sg, dh, dl, wt, wn, seg_all, g, recv_a, recv_b, part = refs[22:33]
    load_sem, seg_send, seg_recv, a_send, a_recv, b_send, b_recv, c_send, c_recv = refs[33:]
    loads = [pltpu.make_async_copy(far[i], near[i], load_sem.at[i]) for i in range(10)]
    for i in (0, 1, 9, 4, 7, 5, 6, 8, 2, 3):
        loads[i].start()
    me = lax.axis_index("slab")
    ray = lax.axis_index("rays")
    core = lax.rem(ray, 2)
    width = geo_ref.shape[2]
    own = tgt_ref.shape[2]
    n = SAMP * width
    hid = win_ref.shape[2]
    fe = fr_ref.shape[2]
    mid = wmid_ref.shape[1]
    layers = mid + 1
    bits = [b for b in range(1, 16) if (1 << b) < n_rays]
    chunk = 256
    n_chunks = n // chunk

    barrier = pltpu.get_barrier_semaphore()
    for k in range(1, slabs):
        pl.semaphore_signal(barrier, inc=1, device_id=(lax.rem(me + k, slabs), ray), device_id_type=MESH)
    peers = [1] + [1 << b for b in bits]

    def other(bit):
        place = lax.rem(ray // bit, 2)
        return ray + bit * (1 - 2 * place)

    for bit in peers:
        pl.semaphore_signal(barrier, inc=1, device_id=(me, other(bit)), device_id_type=MESH)

    def chunks(body):
        if n_chunks <= 4:
            for i in range(n_chunks):
                body(i * chunk)
        else:
            def step(i, carry):
                body(pl.multiple_of(i * chunk, chunk))
                return carry
            lax.fori_loop(0, n_chunks, step, 0)

    for i in (0, 1, 9):
        loads[i].wait()
    freq = jnp.concatenate([fr_ref[:, 0, :], jnp.zeros((5, fe), F32)], axis=0).T

    geo = geo_ref[:, 0, :]
    t0 = 0.25 * (ent_ref[0].astype(F32) + 0.5)
    base = jnp.zeros((fe, width), F32)
    turn = jnp.zeros((fe, width), F32)
    for d in range(3):
        dirs = geo[3 + d:4 + d, :]
        place = geo[d:d + 1, :] + t0 * dirs
        base = base + freq[:, d:d + 1] * place
        turn = turn + freq[:, d:d + 1] * (0.25 * dirs)
    sn, cs = sincos(base)
    sd, cd = sincos(turn)
    for j in range(SAMP):
        lanes = slice(j * width, (j + 1) * width)
        hi, lo = split(sn)
        hx[0, hid:hid + fe, lanes] = hi
        hx[0, 0:fe, lanes] = lo
        hi, lo = split(cs)
        hx[0, hid + fe:hid + 2 * fe, lanes] = hi
        hx[0, fe:2 * fe, lanes] = lo
        if j < SAMP - 1:
            sn, cs = sn * cd + cs * sd, cs * cd - sn * sd

    for i in (2, 3, 4, 5, 6, 7, 8):
        loads[i].wait()
    for l in range(layers):
        hx[l, 2 * hid:2 * hid + 16, :] = jnp.ones((16, n), BF16)
        w = win_ref[0] if l == 0 else wmid_ref[0, l - 1]
        hi, lo = split(w.T)
        wt[l, 0:hid] = hi
        wt[l, hid:2 * hid] = lo
        if l > 0:
            hi, lo = split(w)
            wn[l - 1, 0:hid] = hi
            wn[l - 1, hid:2 * hid] = lo

    pad5 = jnp.zeros((8 - layers, hid), F32)
    bias = jnp.concatenate([bhid_ref[:, 0, :], pad5], axis=0).T

    for l in range(layers):
        def layer(at, l=l):
            lanes = pl.ds(at, chunk)
            both = mm(wt[l], hx[l, hid:2 * hid, lanes])
            z = both[0:hid] + both[hid:2 * hid] + mm(wt[l, 0:hid], hx[l, 0:hid, lanes])
            z = z + bias[:, l:l + 1]
            h = softplus(z)
            sg[l, :, lanes] = jnp.exp(z - h)
            hi, lo = split(h)
            hx[l + 1, hid:2 * hid, lanes] = hi
            hx[l + 1, 0:hid, lanes] = lo
        chunks(layer)

    wo = jnp.concatenate([wout_ref[0], jnp.zeros((4, hid), F32)], axis=0)
    wo_hi, wo_lo = split(wo)
    pair = mm(jnp.concatenate([wo_hi, wo_lo], axis=0), hx[layers, hid:2 * hid, :])
    out = pair[0:8] + pair[8:16] + mm(wo_hi, hx[layers, 0:hid, :])
    bout = jnp.concatenate([bout_ref[...], jnp.zeros((7, 4), F32)], axis=0)
    counts = cnt_ref[0]
    sigma = softplus(out[0:1] + bout[0:1, 0:1])
    sigma_slope = jnp.exp(out[0:1] + bout[0:1, 0:1] - sigma)
    rgb = []
    for c in range(3):
        o = out[c + 1:c + 2] + bout[0:1, c + 1:c + 2]
        rgb.append(jnp.exp(o - softplus(o)))
    rgb = jnp.concatenate(rgb, axis=0)
    before = jnp.zeros((1, width), F32)
    color = jnp.zeros((3, width), F32)
    weight, after, live, tints = [], [], [], []
    for j in range(SAMP):
        lanes = slice(j * width, (j + 1) * width)
        alive = counts > j
        tau = jnp.where(alive, sigma[:, lanes] * delta, 0.0)
        e0 = jnp.exp(-before)
        e1 = jnp.exp(-tau)
        w = e0 * (1.0 - e1)
        tint = rgb[:, lanes]
        color = color + w * tint
        before = before + tau
        weight.append(w)
        after.append(e0 * e1)
        live.append(alive)
        tints.append(tint)
    mine = lax.broadcasted_iota(jnp.int32, (own, width), 1) == (
        lax.broadcasted_iota(jnp.int32, (own, width), 0) + me * own
    )
    spread = jnp.where(mine, 1.0, 0.0).astype(F32)
    spot = jnp.dot(tgt_ref[:, 0, :], spread, precision=lax.Precision.HIGHEST, preferred_element_type=F32)
    seg_all[me] = jnp.concatenate([color, -before, spot, jnp.zeros((1, width), F32)], axis=0)

    pl.semaphore_wait(barrier, slabs - 1 + len(peers))
    copies = []
    for k in range(1, slabs):
        copy = pltpu.make_async_remote_copy(
            src_ref=seg_all.at[me], dst_ref=seg_all.at[me],
            send_sem=seg_send.at[k], recv_sem=seg_recv.at[k],
            device_id=(lax.rem(me + k, slabs), ray), device_id_type=MESH,
        )
        copy.start()
        copies.append(copy)
    for copy in copies:
        copy.wait()

    total = jnp.zeros((1, width), F32)
    pixels = jnp.zeros((3, width), F32)
    target = jnp.zeros((3, width), F32)
    shades, colors = [], []
    mine_shade = jnp.zeros((1, width), F32)
    for s in range(slabs):
        block = seg_all[s]
        shade = jnp.exp(total)
        pixels = pixels + shade * block[0:3]
        target = target + block[4:7]
        total = total + block[3:4]
        mine_shade = mine_shade + jnp.where(me == s, shade, 0.0)
        shades.append(shade)
        colors.append(block[0:3])
    clear = jnp.exp(total)
    pixels = pixels + clear
    pull = (2.0 * factor) * (pixels - target)
    d_log = clear * jnp.sum(pull, axis=0, keepdims=True)
    for s in range(slabs):
        term = shades[s] * jnp.sum(pull * colors[s], axis=0, keepdims=True)
        d_log = d_log + jnp.where(me < s, term, 0.0)
    d_color = mine_shade * pull
    pix_ref[...] = lax.dot_general(
        pixels, spread, NT, precision=lax.Precision.HIGHEST, preferred_element_type=F32
    )

    later = jnp.zeros((1, width), F32)
    d_out = [None] * SAMP
    for j in reversed(range(SAMP)):
        lanes = slice(j * width, (j + 1) * width)
        u = jnp.sum(d_color * tints[j], axis=0, keepdims=True)
        d_tau = after[j] * u - later - d_log
        later = later + weight[j] * u
        d0 = jnp.where(live[j], d_tau * delta * sigma_slope[:, lanes], 0.0)
        d_rgb = d_color * weight[j] * tints[j] * (1.0 - tints[j])
        d_out[j] = jnp.concatenate([d0, d_rgb, jnp.zeros((4, width), F32)], axis=0)
    d_out = jnp.concatenate(d_out, axis=1)
    do_hi, do_lo = split(d_out)
    wot_hi, wot_lo = split(wo.T)

    def last(at):
        lanes = pl.ds(at, chunk)
        hi = dh[1, 0:8, lanes]
        d = mm(wot_hi, hi) + mm(wot_lo, hi) + mm(wot_hi, dl[1, 0:8, lanes])
        hi, lo = split(d * sg[layers - 1, :, lanes])
        dh[0, :, lanes] = hi
        dl[0, :, lanes] = lo

    dh[1, 0:8, :] = do_hi
    dl[1, 0:8, :] = do_lo

    small = hid
    g[layers - 1, small:small + 16, :] = jnp.zeros((16, hid), F32)
    pair = mm_nt(jnp.concatenate([do_hi, do_lo], axis=0), hx[layers, hid:2 * hid, :])
    g_out = pair[0:8] + pair[8:16] + mm_nt(do_hi, hx[layers, 0:hid, :])
    g[layers - 1, small:small + 4, :] = g_out[0:4]
    ones = hx[0, 2 * hid:2 * hid + 16, :]
    row = mm_nt(ones, do_hi) + mm_nt(ones, do_lo)
    g[layers - 1, small + 7:small + 8, 0:8] = row[0:1, 0:8]
    chunks(last)

    def rows_of(b):
        return hid + 16 if b == layers - 1 else hid

    def stage_a(b):
        half = rows_of(b) // 2
        return pltpu.make_async_remote_copy(
            src_ref=g.at[b, pl.ds(pl.multiple_of((1 - core) * half, 8), half)],
            dst_ref=recv_a.at[b, pl.ds(0, half)],
            send_sem=a_send.at[b], recv_sem=a_recv.at[b],
            device_id=(me, other(1)), device_id_type=MESH,
        )

    def stage_b(b, i):
        half = rows_of(b) // 2
        return pltpu.make_async_remote_copy(
            src_ref=part.at[b, i, pl.ds(0, half)], dst_ref=recv_b.at[b, i, pl.ds(0, half)],
            send_sem=b_send.at[b, i], recv_sem=b_recv.at[b, i],
            device_id=(me, other(1 << bits[i])), device_id_type=MESH,
        )

    def stage_c(b):
        half = rows_of(b) // 2
        rows = pl.ds(pl.multiple_of(core * half, 8), half)
        return pltpu.make_async_remote_copy(
            src_ref=fin.at[b, rows], dst_ref=fin.at[b, rows],
            send_sem=c_send.at[b], recv_sem=c_recv.at[b],
            device_id=(me, other(1)), device_id_type=MESH,
        )

    def after_a(b):
        half = rows_of(b) // 2
        stage_a(b).wait()
        value = g[b, pl.ds(pl.multiple_of(core * half, 8), half), :] + recv_a[b, 0:half, :]
        if bits:
            part[b, 0, 0:half, :] = value
            stage_b(b, 0).start()
        else:
            fin[b, pl.ds(pl.multiple_of(core * half, 8), half), :] = value
            stage_c(b).start()

    def after_b(b, i):
        half = rows_of(b) // 2
        stage_b(b, i).wait()
        value = part[b, i, 0:half, :] + recv_b[b, i, 0:half, :]
        if i + 1 < len(bits):
            part[b, i + 1, 0:half, :] = value
            stage_b(b, i + 1).start()
        else:
            fin[b, pl.ds(pl.multiple_of(core * half, 8), half), :] = value
            stage_c(b).start()

    steps = []
    for b in range(layers):
        steps.append([functools.partial(after_a, b)] + [functools.partial(after_b, b, i) for i in range(len(bits))])

    for b in range(layers):
        l = layers - 1 - b
        slot = b % 2
        dz_hi, dz_lo = dh[slot], dl[slot]
        first = mm_nt(hx[l], dz_hi)
        second = mm_nt(hx[l, hid:2 * hid + 16], dz_lo)
        bias_row = first[2 * hid:2 * hid + 16] + second[hid:hid + 16]
        g[b, 0:hid, :] = first[0:hid] + first[hid:2 * hid] + second[0:hid]
        g[layers - 1, small + 4 + l:small + 5 + l, :] = bias_row[0:1]
        stage_a(b).start()
        for earlier in range(b):
            if steps[earlier]:
                steps[earlier].pop(0)()
        if l > 0:
            def back(at, l=l, slot=slot):
                lanes = pl.ds(at, chunk)
                both = mm(wn[l - 1], dh[slot, :, lanes])
                d = both[0:hid] + both[hid:2 * hid] + mm(wn[l - 1, 0:hid], dl[slot, :, lanes])
                hi, lo = split(d * sg[l - 1, :, lanes])
                dh[1 - slot, :, lanes] = hi
                dl[1 - slot, :, lanes] = lo
            chunks(back)
            if steps[b]:
                steps[b].pop(0)()
    while any(steps):
        for b in range(layers):
            if steps[b]:
                steps[b].pop(0)()
    for b in range(layers):
        stage_c(b).wait()


def unpack(pix_in, fin, pix_ref, gin_ref, gmid_ref, gout_ref, ghid_ref, gbout_ref, sems):
    layers = fin.shape[0]
    hid = fin.shape[2]
    copies = []
    for l in range(layers):
        place = gin_ref.at[0] if l == 0 else gmid_ref.at[0, l - 1]
        copies.append(pltpu.make_async_copy(fin.at[layers - 1 - l, pl.ds(0, hid)], place, sems.at[l]))
    for copy in copies:
        copy.start()
    tail = fin[layers - 1, hid:hid + 16, :]
    gout_ref[0] = tail[0:4]
    ghid_ref[:, 0, :] = tail[4:4 + layers]
    gbout_ref[...] = tail[7:8, 0:4]
    pix_ref[:, 0, :] = pix_in[0:3, :]
    for copy in copies:
        copy.wait()


def solution(mesh):
    slabs, n_rays = mesh.shape["slab"], mesh.shape["rays"]

    def shards(geometry, entry, counts, targets, w_in, w_mid, w_out, b_hid, b_out, freqs):
        width = geometry.shape[2]
        own = targets.shape[2]
        n = SAMP * width
        hid = w_in.shape[2]
        mid = w_mid.shape[1]
        layers = mid + 1
        delta = 3.0 / (SAMP * slabs)
        factor = 1.0 / math.sqrt(3.0 * n_rays * slabs * own)
        more = max(1, sum(1 for b in range(1, 16) if (1 << b) < n_rays))
        half = (hid + 16) // 2
        shape = jax.ShapeDtypeStruct
        args = (
            geometry, entry, counts, targets, w_in, w_mid, w_out,
            jnp.transpose(b_hid, (1, 0, 2)), b_out, jnp.transpose(freqs, (1, 0, 2)),
        )
        vmem = pl.BlockSpec(memory_space=pltpu.VMEM)
        pixels, packed = pl.pallas_call(
            functools.partial(kernel, slabs, n_rays, delta, factor),
            out_shape=(pltpu.VMEM((3, own), F32), pltpu.VMEM((layers, hid + 16, hid), F32)),
            in_specs=[pl.BlockSpec(memory_space=pltpu.HBM)] * 10,
            out_specs=(vmem, vmem),
            scratch_shapes=[pltpu.VMEM(a.shape, a.dtype) for a in args] + [
                pltpu.VMEM((layers + 1, 2 * hid + 16, n), BF16),
                pltpu.VMEM((layers, hid, n), F32),
                pltpu.VMEM((2, hid, n), BF16),
                pltpu.VMEM((2, hid, n), BF16),
                pltpu.VMEM((layers, 2 * hid, hid), BF16),
                pltpu.VMEM((mid, 2 * hid, hid), BF16),
                pltpu.VMEM((slabs, 8, width), F32),
                pltpu.VMEM((layers, hid + 16, hid), F32),
                pltpu.VMEM((layers, half, hid), F32),
                pltpu.VMEM((layers, more, half, hid), F32),
                pltpu.VMEM((layers, more, half, hid), F32),
                pltpu.SemaphoreType.DMA((10,)),
                pltpu.SemaphoreType.DMA((slabs,)),
                pltpu.SemaphoreType.DMA((slabs,)),
                pltpu.SemaphoreType.DMA((layers,)),
                pltpu.SemaphoreType.DMA((layers,)),
                pltpu.SemaphoreType.DMA((layers, more)),
                pltpu.SemaphoreType.DMA((layers, more)),
                pltpu.SemaphoreType.DMA((layers,)),
                pltpu.SemaphoreType.DMA((layers,)),
            ],
            compiler_params=pltpu.CompilerParams(
                collective_id=0, has_side_effects=True, vmem_limit_bytes=58 * 1000 * 1024
            ),
        )(*args)
        hbm = pl.BlockSpec(memory_space=pltpu.HBM)
        outs = pl.pallas_call(
            unpack,
            out_shape=(
                shape((3, 1, own), F32),
                shape((1, 2 * freqs.shape[2], hid), F32),
                shape((1, mid, hid, hid), F32),
                shape((1, 4, hid), F32),
                shape((layers, 1, hid), F32),
                shape((1, 4), F32),
            ),
            in_specs=[vmem] * 2,
            out_specs=(vmem, hbm, hbm, vmem, vmem, vmem),
            scratch_shapes=[pltpu.SemaphoreType.DMA((layers,))],
            compiler_params=pltpu.CompilerParams(vmem_limit_bytes=8 << 20),
        )(pixels, packed)
        return outs[:4] + (jnp.transpose(outs[4], (1, 0, 2)), outs[5])

    in_specs = (
        P(None, "rays", None),
        P("slab", "rays", None),
        P("slab", "rays", None),
        P(None, "rays", "slab"),
        P("slab", None, None),
        P("slab", None, None, None),
        P("slab", None, None),
        P("slab", None, None),
        P("slab", None),
        P("slab", None, None),
    )
    out_specs = (
        P(None, "rays", "slab"),
        P("slab", None, None),
        P("slab", None, None, None),
        P("slab", None, None),
        P("slab", None, None),
        P("slab", None),
    )
    return jax.shard_map(shards, mesh=mesh, in_specs=in_specs, out_specs=out_specs, check_vma=False)
```

```python
import functools
import math

import jax
import jax.numpy as jnp
from jax import lax
from jax.experimental import pallas as pl
from jax.experimental.pallas import tpu as pltpu
from jax.sharding import PartitionSpec as P

SAMP = 8
F32 = jnp.float32
PIECES = 2
BF16 = jnp.bfloat16
MESH = pl.DeviceIdType.MESH
NT = (((1,), (1,)), ((), ()))


def split(x):
    hi = x.astype(BF16)
    return hi, (x - hi.astype(F32)).astype(BF16)


def mm(a, b):
    return jnp.dot(a, b, preferred_element_type=F32)


def mm_nt(a, b):
    return lax.dot_general(a, b, NT, preferred_element_type=F32)


def softplus(z):
    return jnp.maximum(z, 0.0) + jnp.log1p(jnp.exp(-jnp.abs(z)))


def sincos(x):
    k = jnp.round(x * F32(2.0 / math.pi))
    r = ((x - k * F32(1.5703125)) - k * F32(4.837512969970703e-4)) - k * F32(7.549789954891882e-8)
    q = k.astype(jnp.int32)
    r2 = r * r
    s = r + r * r2 * (F32(-1.6666654611e-1) + r2 * (F32(8.3321608736e-3) + r2 * F32(-1.9515295891e-4)))
    c = F32(1.0) - F32(0.5) * r2 + r2 * r2 * (
        F32(4.166664568298827e-2) + r2 * (F32(-1.388731625493765e-3) + r2 * F32(2.443315711809948e-5))
    )
    odd = (q & 1) == 1
    sn = jnp.where(odd, c, s)
    cs = jnp.where(odd, s, c)
    sn = jnp.where((q & 2) == 2, -sn, sn)
    cs = jnp.where(((q + 1) & 2) == 2, -cs, cs)
    return sn, cs


def kernel(
    slabs, n_rays, delta, factor,
    *refs,
):
    far, (pix_ref, fin), near = refs[:10], refs[10:12], refs[12:22]
    geo_ref, ent_ref, cnt_ref, tgt_ref, win_ref, wmid_ref, wout_ref, bhid_ref, bout_ref, fr_ref = near
    hx, sg, dh, dl, wt, wn, seg_all, g, recv_a, recv_b, part = refs[22:33]
    load_sem, seg_send, seg_recv, a_send, a_recv, b_send, b_recv, c_send, c_recv = refs[33:]
    loads = [pltpu.make_async_copy(far[i], near[i], load_sem.at[i]) for i in range(10)]
    for i in (0, 1, 9, 4, 7, 5, 6, 8, 2, 3):
        loads[i].start()
    me = lax.axis_index("slab")
    ray = lax.axis_index("rays")
    core = lax.rem(ray, 2)
    width = geo_ref.shape[2]
    own = tgt_ref.shape[2]
    n = SAMP * width
    hid = win_ref.shape[2]
    fe = fr_ref.shape[2]
    mid = wmid_ref.shape[1]
    layers = mid + 1
    bits = [b for b in range(1, 16) if (1 << b) < n_rays]
    chunk = 256
    n_chunks = n // chunk

    barrier = pltpu.get_barrier_semaphore()
    for k in range(1, slabs):
        pl.semaphore_signal(barrier, inc=1, device_id=(lax.rem(me + k, slabs), ray), device_id_type=MESH)
    peers = [1] + [1 << b for b in bits]

    def other(bit):
        place = lax.rem(ray // bit, 2)
        return ray + bit * (1 - 2 * place)

    for bit in peers:
        pl.semaphore_signal(barrier, inc=1, device_id=(me, other(bit)), device_id_type=MESH)

    def chunks(body):
        if n_chunks <= 4:
            for i in range(n_chunks):
                body(i * chunk)
        else:
            def step(i, carry):
                body(pl.multiple_of(i * chunk, chunk))
                return carry
            lax.fori_loop(0, n_chunks, step, 0)

    for i in (0, 1, 9):
        loads[i].wait()
    freq = jnp.concatenate([fr_ref[:, 0, :], jnp.zeros((5, fe), F32)], axis=0).T

    geo = geo_ref[:, 0, :]
    t0 = 0.25 * (ent_ref[0].astype(F32) + 0.5)
    base = jnp.zeros((fe, width), F32)
    turn = jnp.zeros((fe, width), F32)
    for d in range(3):
        dirs = geo[3 + d:4 + d, :]
        place = geo[d:d + 1, :] + t0 * dirs
        base = base + freq[:, d:d + 1] * place
        turn = turn + freq[:, d:d + 1] * (0.25 * dirs)
    sn, cs = sincos(base)
    sd, cd = sincos(turn)
    for j in range(SAMP):
        lanes = slice(j * width, (j + 1) * width)
        hi, lo = split(sn)
        hx[0, hid:hid + fe, lanes] = hi
        hx[0, 0:fe, lanes] = lo
        hi, lo = split(cs)
        hx[0, hid + fe:hid + 2 * fe, lanes] = hi
        hx[0, fe:2 * fe, lanes] = lo
        if j < SAMP - 1:
            sn, cs = sn * cd + cs * sd, cs * cd - sn * sd

    for i in (2, 3, 4, 5, 6, 7, 8):
        loads[i].wait()
    for l in range(layers):
        hx[l, 2 * hid:2 * hid + 16, :] = jnp.ones((16, n), BF16)
        w = win_ref[0] if l == 0 else wmid_ref[0, l - 1]
        hi, lo = split(w.T)
        wt[l, 0:hid] = hi
        wt[l, hid:2 * hid] = lo
        if l > 0:
            hi, lo = split(w)
            wn[l - 1, 0:hid] = hi
            wn[l - 1, hid:2 * hid] = lo

    pad5 = jnp.zeros((8 - layers, hid), F32)
    bias = jnp.concatenate([bhid_ref[:, 0, :], pad5], axis=0).T

    for l in range(layers):
        def layer(at, l=l):
            lanes = pl.ds(at, chunk)
            both = mm(wt[l], hx[l, hid:2 * hid, lanes])
            z = both[0:hid] + both[hid:2 * hid] + mm(wt[l, 0:hid], hx[l, 0:hid, lanes])
            z = z + bias[:, l:l + 1]
            h = softplus(z)
            sg[l, :, lanes] = jnp.exp(z - h)
            hi, lo = split(h)
            hx[l + 1, hid:2 * hid, lanes] = hi
            hx[l + 1, 0:hid, lanes] = lo
        chunks(layer)

    wo = jnp.concatenate([wout_ref[0], jnp.zeros((4, hid), F32)], axis=0)
    wo_hi, wo_lo = split(wo)
    pair = mm(jnp.concatenate([wo_hi, wo_lo], axis=0), hx[layers, hid:2 * hid, :])
    out = pair[0:8] + pair[8:16] + mm(wo_hi, hx[layers, 0:hid, :])
    bout = jnp.concatenate([bout_ref[...], jnp.zeros((7, 4), F32)], axis=0)
    counts = cnt_ref[0]
    sigma = softplus(out[0:1] + bout[0:1, 0:1])
    sigma_slope = jnp.exp(out[0:1] + bout[0:1, 0:1] - sigma)
    rgb = []
    for c in range(3):
        o = out[c + 1:c + 2] + bout[0:1, c + 1:c + 2]
        rgb.append(jnp.exp(o - softplus(o)))
    rgb = jnp.concatenate(rgb, axis=0)
    before = jnp.zeros((1, width), F32)
    color = jnp.zeros((3, width), F32)
    weight, after, live, tints = [], [], [], []
    for j in range(SAMP):
        lanes = slice(j * width, (j + 1) * width)
        alive = counts > j
        tau = jnp.where(alive, sigma[:, lanes] * delta, 0.0)
        e0 = jnp.exp(-before)
        e1 = jnp.exp(-tau)
        w = e0 * (1.0 - e1)
        tint = rgb[:, lanes]
        color = color + w * tint
        before = before + tau
        weight.append(w)
        after.append(e0 * e1)
        live.append(alive)
        tints.append(tint)
    mine = lax.broadcasted_iota(jnp.int32, (own, width), 1) == (
        lax.broadcasted_iota(jnp.int32, (own, width), 0) + me * own
    )
    spread = jnp.where(mine, 1.0, 0.0).astype(F32)
    spot = jnp.dot(tgt_ref[:, 0, :], spread, precision=lax.Precision.HIGHEST, preferred_element_type=F32)
    seg_all[me] = jnp.concatenate([color, -before, spot, jnp.zeros((1, width), F32)], axis=0)

    pl.semaphore_wait(barrier, slabs - 1 + len(peers))
    copies = []
    for k in range(1, slabs):
        copy = pltpu.make_async_remote_copy(
            src_ref=seg_all.at[me], dst_ref=seg_all.at[me],
            send_sem=seg_send.at[k], recv_sem=seg_recv.at[k],
            device_id=(lax.rem(me + k, slabs), ray), device_id_type=MESH,
        )
        copy.start()
        copies.append(copy)
    for copy in copies:
        copy.wait()

    total = jnp.zeros((1, width), F32)
    pixels = jnp.zeros((3, width), F32)
    target = jnp.zeros((3, width), F32)
    shades, colors = [], []
    mine_shade = jnp.zeros((1, width), F32)
    for s in range(slabs):
        block = seg_all[s]
        shade = jnp.exp(total)
        pixels = pixels + shade * block[0:3]
        target = target + block[4:7]
        total = total + block[3:4]
        mine_shade = mine_shade + jnp.where(me == s, shade, 0.0)
        shades.append(shade)
        colors.append(block[0:3])
    clear = jnp.exp(total)
    pixels = pixels + clear
    pull = (2.0 * factor) * (pixels - target)
    d_log = clear * jnp.sum(pull, axis=0, keepdims=True)
    for s in range(slabs):
        term = shades[s] * jnp.sum(pull * colors[s], axis=0, keepdims=True)
        d_log = d_log + jnp.where(me < s, term, 0.0)
    d_color = mine_shade * pull
    pix_ref[...] = lax.dot_general(
        pixels, spread, NT, precision=lax.Precision.HIGHEST, preferred_element_type=F32
    )

    later = jnp.zeros((1, width), F32)
    d_out = [None] * SAMP
    for j in reversed(range(SAMP)):
        lanes = slice(j * width, (j + 1) * width)
        u = jnp.sum(d_color * tints[j], axis=0, keepdims=True)
        d_tau = after[j] * u - later - d_log
        later = later + weight[j] * u
        d0 = jnp.where(live[j], d_tau * delta * sigma_slope[:, lanes], 0.0)
        d_rgb = d_color * weight[j] * tints[j] * (1.0 - tints[j])
        d_out[j] = jnp.concatenate([d0, d_rgb, jnp.zeros((4, width), F32)], axis=0)
    d_out = jnp.concatenate(d_out, axis=1)
    do_hi, do_lo = split(d_out)
    wot_hi, wot_lo = split(wo.T)

    def last(at):
        lanes = pl.ds(at, chunk)
        hi = dh[1, 0:8, lanes]
        d = mm(wot_hi, hi) + mm(wot_lo, hi) + mm(wot_hi, dl[1, 0:8, lanes])
        hi, lo = split(d * sg[layers - 1, :, lanes])
        dh[0, :, lanes] = hi
        dl[0, :, lanes] = lo

    dh[1, 0:8, :] = do_hi
    dl[1, 0:8, :] = do_lo

    small = hid
    g[layers - 1, small:small + 32, :] = jnp.zeros((32, hid), F32)

    def head_grads():
        pair = mm_nt(jnp.concatenate([do_hi, do_lo], axis=0), hx[layers, hid:2 * hid, :])
        g_out = pair[0:8] + pair[8:16] + mm_nt(do_hi, hx[layers, 0:hid, :])
        g[layers - 1, small:small + 4, :] = g_out[0:4]
        ones = hx[0, 2 * hid:2 * hid + 16, :]
        row = mm_nt(ones, do_hi) + mm_nt(ones, do_lo)
        g[layers - 1, small + 7:small + 8, 0:8] = row[0:1, 0:8]

    chunks(last)

    def rows_of(b):
        return hid + 32 if b == layers - 1 else hid

    def piece(b):
        return rows_of(b) // 2 // PIECES

    def at_core(b, p, which):
        return pl.ds(pl.multiple_of(which * (rows_of(b) // 2) + p * piece(b), 8), piece(b))

    def stage_a(b, p):
        return pltpu.make_async_remote_copy(
            src_ref=g.at[b, at_core(b, p, 1 - core)],
            dst_ref=recv_a.at[b, pl.ds(p * piece(b), piece(b))],
            send_sem=a_send.at[b, p], recv_sem=a_recv.at[b, p],
            device_id=(me, other(1)), device_id_type=MESH,
        )

    def stage_b(b, i, p):
        rows = pl.ds(p * piece(b), piece(b))
        return pltpu.make_async_remote_copy(
            src_ref=part.at[b, i, rows], dst_ref=recv_b.at[b, i, rows],
            send_sem=b_send.at[b, i, p], recv_sem=b_recv.at[b, i, p],
            device_id=(me, other(1 << bits[i])), device_id_type=MESH,
        )

    def stage_c(b, p):
        rows = at_core(b, p, core)
        return pltpu.make_async_remote_copy(
            src_ref=fin.at[b, rows], dst_ref=fin.at[b, rows],
            send_sem=c_send.at[b, p], recv_sem=c_recv.at[b, p],
            device_id=(me, other(1)), device_id_type=MESH,
        )

    def send_on(b, i, p, value):
        if i < len(bits):
            part[b, i, p * piece(b):(p + 1) * piece(b), :] = value
            stage_b(b, i, p).start()
        else:
            fin[b, at_core(b, p, core), :] = value
            stage_c(b, p).start()

    def after_a(b):
        for p in range(PIECES):
            stage_a(b, p).wait()
            send_on(b, 0, p, g[b, at_core(b, p, core), :] + recv_a[b, p * piece(b):(p + 1) * piece(b), :])

    def after_b(b, i):
        for p in range(PIECES):
            rows = slice(p * piece(b), (p + 1) * piece(b))
            stage_b(b, i, p).wait()
            send_on(b, i + 1, p, part[b, i, rows, :] + recv_b[b, i, rows, :])

    steps = []
    for b in range(layers):
        steps.append([functools.partial(after_a, b)] + [functools.partial(after_b, b, i) for i in range(len(bits))])

    for b in range(layers):
        l = layers - 1 - b
        slot = b % 2
        dz_hi, dz_lo = dh[slot], dl[slot]
        first = mm_nt(hx[l], dz_hi)
        second = mm_nt(hx[l, hid:2 * hid + 16], dz_lo)
        bias_row = first[2 * hid:2 * hid + 16] + second[hid:hid + 16]
        g[b, 0:hid, :] = first[0:hid] + first[hid:2 * hid] + second[0:hid]
        g[layers - 1, small + 4 + l:small + 5 + l, :] = bias_row[0:1]
        for p in range(PIECES):
            stage_a(b, p).start()
        if b == 0:
            head_grads()
        for earlier in range(b):
            if steps[earlier]:
                steps[earlier].pop(0)()
        if l > 0:
            def back(at, l=l, slot=slot):
                lanes = pl.ds(at, chunk)
                both = mm(wn[l - 1], dh[slot, :, lanes])
                d = both[0:hid] + both[hid:2 * hid] + mm(wn[l - 1, 0:hid], dl[slot, :, lanes])
                hi, lo = split(d * sg[l - 1, :, lanes])
                dh[1 - slot, :, lanes] = hi
                dl[1 - slot, :, lanes] = lo
            chunks(back)
            if steps[b]:
                steps[b].pop(0)()
    while any(steps):
        for b in range(layers):
            if steps[b]:
                steps[b].pop(0)()
    for b in range(layers):
        for p in range(PIECES):
            stage_c(b, p).wait()


def unpack(pix_in, fin, pix_ref, gin_ref, gmid_ref, gout_ref, ghid_ref, gbout_ref, sems):
    layers = fin.shape[0]
    hid = fin.shape[2]
    copies = []
    for l in range(layers):
        place = gin_ref.at[0] if l == 0 else gmid_ref.at[0, l - 1]
        copies.append(pltpu.make_async_copy(fin.at[layers - 1 - l, pl.ds(0, hid)], place, sems.at[l]))
    for copy in copies:
        copy.start()
    tail = fin[layers - 1, hid:hid + 16, :]
    gout_ref[0] = tail[0:4]
    ghid_ref[:, 0, :] = tail[4:4 + layers]
    gbout_ref[...] = tail[7:8, 0:4]
    pix_ref[:, 0, :] = pix_in[0:3, :]
    for copy in copies:
        copy.wait()


def solution(mesh):
    slabs, n_rays = mesh.shape["slab"], mesh.shape["rays"]

    def shards(geometry, entry, counts, targets, w_in, w_mid, w_out, b_hid, b_out, freqs):
        width = geometry.shape[2]
        own = targets.shape[2]
        n = SAMP * width
        hid = w_in.shape[2]
        mid = w_mid.shape[1]
        layers = mid + 1
        delta = 3.0 / (SAMP * slabs)
        factor = 1.0 / math.sqrt(3.0 * n_rays * slabs * own)
        more = max(1, sum(1 for b in range(1, 16) if (1 << b) < n_rays))
        half = (hid + 32) // 2
        shape = jax.ShapeDtypeStruct
        args = (
            geometry, entry, counts, targets, w_in, w_mid, w_out,
            jnp.transpose(b_hid, (1, 0, 2)), b_out, jnp.transpose(freqs, (1, 0, 2)),
        )
        vmem = pl.BlockSpec(memory_space=pltpu.VMEM)
        pixels, packed = pl.pallas_call(
            functools.partial(kernel, slabs, n_rays, delta, factor),
            out_shape=(pltpu.VMEM((3, own), F32), pltpu.VMEM((layers, hid + 32, hid), F32)),
            in_specs=[pl.BlockSpec(memory_space=pltpu.HBM)] * 10,
            out_specs=(vmem, vmem),
            scratch_shapes=[pltpu.VMEM(a.shape, a.dtype) for a in args] + [
                pltpu.VMEM((layers + 1, 2 * hid + 16, n), BF16),
                pltpu.VMEM((layers, hid, n), F32),
                pltpu.VMEM((2, hid, n), BF16),
                pltpu.VMEM((2, hid, n), BF16),
                pltpu.VMEM((layers, 2 * hid, hid), BF16),
                pltpu.VMEM((mid, 2 * hid, hid), BF16),
                pltpu.VMEM((slabs, 8, width), F32),
                pltpu.VMEM((layers, hid + 32, hid), F32),
                pltpu.VMEM((layers, half, hid), F32),
                pltpu.VMEM((layers, more, half, hid), F32),
                pltpu.VMEM((layers, more, half, hid), F32),
                pltpu.SemaphoreType.DMA((10,)),
                pltpu.SemaphoreType.DMA((slabs,)),
                pltpu.SemaphoreType.DMA((slabs,)),
                pltpu.SemaphoreType.DMA((layers, PIECES)),
                pltpu.SemaphoreType.DMA((layers, PIECES)),
                pltpu.SemaphoreType.DMA((layers, more, PIECES)),
                pltpu.SemaphoreType.DMA((layers, more, PIECES)),
                pltpu.SemaphoreType.DMA((layers, PIECES)),
                pltpu.SemaphoreType.DMA((layers, PIECES)),
            ],
            compiler_params=pltpu.CompilerParams(
                collective_id=0, has_side_effects=True, vmem_limit_bytes=58 * 1000 * 1024
            ),
        )(*args)
        hbm = pl.BlockSpec(memory_space=pltpu.HBM)
        outs = pl.pallas_call(
            unpack,
            out_shape=(
                shape((3, 1, own), F32),
                shape((1, 2 * freqs.shape[2], hid), F32),
                shape((1, mid, hid, hid), F32),
                shape((1, 4, hid), F32),
                shape((layers, 1, hid), F32),
                shape((1, 4), F32),
            ),
            in_specs=[vmem] * 2,
            out_specs=(vmem, hbm, hbm, vmem, vmem, vmem),
            scratch_shapes=[pltpu.SemaphoreType.DMA((layers,))],
            compiler_params=pltpu.CompilerParams(vmem_limit_bytes=8 << 20),
        )(pixels, packed)
        return outs[:4] + (jnp.transpose(outs[4], (1, 0, 2)), outs[5])

    in_specs = (
        P(None, "rays", None),
        P("slab", "rays", None),
        P("slab", "rays", None),
        P(None, "rays", "slab"),
        P("slab", None, None),
        P("slab", None, None, None),
        P("slab", None, None),
        P("slab", None, None),
        P("slab", None),
        P("slab", None, None),
    )
    out_specs = (
        P(None, "rays", "slab"),
        P("slab", None, None),
        P("slab", None, None, None),
        P("slab", None, None),
        P("slab", None, None),
        P("slab", None),
    )
    return jax.shard_map(shards, mesh=mesh, in_specs=in_specs, out_specs=out_specs, check_vma=False)
```

```python
import functools
import math

import jax
import jax.numpy as jnp
from jax import lax
from jax.experimental import pallas as pl
from jax.experimental.pallas import tpu as pltpu
from jax.sharding import PartitionSpec as P

SAMP = 8
F32 = jnp.float32
PIECES = 2
BF16 = jnp.bfloat16
MESH = pl.DeviceIdType.MESH
NT = (((1,), (1,)), ((), ()))


def split(x):
    hi = x.astype(BF16)
    return hi, (x - hi.astype(F32)).astype(BF16)


def mm(a, b):
    return jnp.dot(a, b, preferred_element_type=F32)


def mm_nt(a, b):
    return lax.dot_general(a, b, NT, preferred_element_type=F32)


def softplus(z):
    return jnp.maximum(z, 0.0) + jnp.log1p(jnp.exp(-jnp.abs(z)))


def sincos(x):
    k = jnp.round(x * F32(2.0 / math.pi))
    r = ((x - k * F32(1.5703125)) - k * F32(4.837512969970703e-4)) - k * F32(7.549789954891882e-8)
    q = k.astype(jnp.int32)
    r2 = r * r
    s = r + r * r2 * (F32(-1.6666654611e-1) + r2 * (F32(8.3321608736e-3) + r2 * F32(-1.9515295891e-4)))
    c = F32(1.0) - F32(0.5) * r2 + r2 * r2 * (
        F32(4.166664568298827e-2) + r2 * (F32(-1.388731625493765e-3) + r2 * F32(2.443315711809948e-5))
    )
    odd = (q & 1) == 1
    sn = jnp.where(odd, c, s)
    cs = jnp.where(odd, s, c)
    sn = jnp.where((q & 2) == 2, -sn, sn)
    cs = jnp.where(((q + 1) & 2) == 2, -cs, cs)
    return sn, cs


def kernel(
    slabs, n_rays, delta, factor,
    *refs,
):
    far, (pix_ref, fin), near = refs[:10], refs[10:12], refs[12:22]
    geo_ref, ent_ref, cnt_ref, tgt_ref, win_ref, wmid_ref, wout_ref, bhid_ref, bout_ref, fr_ref = near
    hx, sg, dh, dl, wt, wn, seg_all, g, recv_a, recv_b, part = refs[22:33]
    load_sem, seg_send, seg_recv, a_send, a_recv, b_send, b_recv, c_send, c_recv = refs[33:]
    loads = [pltpu.make_async_copy(far[i], near[i], load_sem.at[i]) for i in range(10)]
    for i in (0, 1, 9, 4, 7, 5, 6, 8, 2, 3):
        loads[i].start()
    me = lax.axis_index("slab")
    ray = lax.axis_index("rays")
    core = lax.rem(ray, 2)
    width = geo_ref.shape[2]
    own = tgt_ref.shape[2]
    n = SAMP * width
    hid = win_ref.shape[2]
    fe = fr_ref.shape[2]
    mid = wmid_ref.shape[1]
    layers = mid + 1
    bits = [b for b in range(1, 16) if (1 << b) < n_rays]
    chunk = 256
    n_chunks = n // chunk

    barrier = pltpu.get_barrier_semaphore()
    for k in range(1, slabs):
        pl.semaphore_signal(barrier, inc=1, device_id=(lax.rem(me + k, slabs), ray), device_id_type=MESH)
    peers = [1] + [1 << b for b in bits]

    def other(bit):
        place = lax.rem(ray // bit, 2)
        return ray + bit * (1 - 2 * place)

    for bit in peers:
        pl.semaphore_signal(barrier, inc=1, device_id=(me, other(bit)), device_id_type=MESH)

    def chunks(body):
        if n_chunks <= 4:
            for i in range(n_chunks):
                body(i * chunk)
        else:
            def step(i, carry):
                body(pl.multiple_of(i * chunk, chunk))
                return carry
            lax.fori_loop(0, n_chunks, step, 0)

    for i in (0, 1, 9):
        loads[i].wait()
    freq = jnp.concatenate([fr_ref[:, 0, :], jnp.zeros((5, fe), F32)], axis=0).T

    geo = geo_ref[:, 0, :]
    t0 = 0.25 * (ent_ref[0].astype(F32) + 0.5)
    base = jnp.zeros((fe, width), F32)
    turn = jnp.zeros((fe, width), F32)
    for d in range(3):
        dirs = geo[3 + d:4 + d, :]
        place = geo[d:d + 1, :] + t0 * dirs
        base = base + freq[:, d:d + 1] * place
        turn = turn + freq[:, d:d + 1] * (0.25 * dirs)
    sn, cs = sincos(base)
    sd, cd = sincos(turn)
    for j in range(SAMP):
        lanes = slice(j * width, (j + 1) * width)
        hi, lo = split(sn)
        hx[0, hid:hid + fe, lanes] = hi
        hx[0, 0:fe, lanes] = lo
        hi, lo = split(cs)
        hx[0, hid + fe:hid + 2 * fe, lanes] = hi
        hx[0, fe:2 * fe, lanes] = lo
        if j < SAMP - 1:
            sn, cs = sn * cd + cs * sd, cs * cd - sn * sd

    for i in (2, 3, 4, 5, 6, 7, 8):
        loads[i].wait()
    for l in range(layers):
        hx[l, 2 * hid:2 * hid + 16, :] = jnp.ones((16, n), BF16)
        w = win_ref[0] if l == 0 else wmid_ref[0, l - 1]
        hi, lo = split(w.T)
        wt[l, 0:hid] = hi
        wt[l, hid:2 * hid] = lo
        if l > 0:
            hi, lo = split(w)
            wn[l - 1, 0:hid] = hi
            wn[l - 1, hid:2 * hid] = lo

    pad5 = jnp.zeros((8 - layers, hid), F32)
    bias = jnp.concatenate([bhid_ref[:, 0, :], pad5], axis=0).T

    for l in range(layers):
        def layer(at, l=l):
            lanes = pl.ds(at, chunk)
            both = mm(wt[l], hx[l, hid:2 * hid, lanes])
            z = both[0:hid] + both[hid:2 * hid] + mm(wt[l, 0:hid], hx[l, 0:hid, lanes])
            z = z + bias[:, l:l + 1]
            h = softplus(z)
            sg[l, :, lanes] = jnp.exp(z - h)
            hi, lo = split(h)
            hx[l + 1, hid:2 * hid, lanes] = hi
            hx[l + 1, 0:hid, lanes] = lo
        chunks(layer)

    wo = jnp.concatenate([wout_ref[0], jnp.zeros((4, hid), F32)], axis=0)
    wo_hi, wo_lo = split(wo)
    pair = mm(jnp.concatenate([wo_hi, wo_lo], axis=0), hx[layers, hid:2 * hid, :])
    out = pair[0:8] + pair[8:16] + mm(wo_hi, hx[layers, 0:hid, :])
    bout = jnp.concatenate([bout_ref[...], jnp.zeros((7, 4), F32)], axis=0)
    counts = cnt_ref[0]
    sigma = softplus(out[0:1] + bout[0:1, 0:1])
    sigma_slope = jnp.exp(out[0:1] + bout[0:1, 0:1] - sigma)
    rgb = []
    for c in range(3):
        o = out[c + 1:c + 2] + bout[0:1, c + 1:c + 2]
        rgb.append(jnp.exp(o - softplus(o)))
    rgb = jnp.concatenate(rgb, axis=0)
    before = jnp.zeros((1, width), F32)
    color = jnp.zeros((3, width), F32)
    weight, after, live, tints = [], [], [], []
    for j in range(SAMP):
        lanes = slice(j * width, (j + 1) * width)
        alive = counts > j
        tau = jnp.where(alive, sigma[:, lanes] * delta, 0.0)
        e0 = jnp.exp(-before)
        e1 = jnp.exp(-tau)
        w = e0 * (1.0 - e1)
        tint = rgb[:, lanes]
        color = color + w * tint
        before = before + tau
        weight.append(w)
        after.append(e0 * e1)
        live.append(alive)
        tints.append(tint)
    mine = lax.broadcasted_iota(jnp.int32, (own, width), 1) == (
        lax.broadcasted_iota(jnp.int32, (own, width), 0) + me * own
    )
    spread = jnp.where(mine, 1.0, 0.0).astype(F32)
    spot = jnp.dot(tgt_ref[:, 0, :], spread, precision=lax.Precision.HIGHEST, preferred_element_type=F32)
    seg_all[me] = jnp.concatenate([color, -before, spot, jnp.zeros((1, width), F32)], axis=0)

    pl.semaphore_wait(barrier, slabs - 1 + len(peers))
    copies = []
    for k in range(1, slabs):
        copy = pltpu.make_async_remote_copy(
            src_ref=seg_all.at[me], dst_ref=seg_all.at[me],
            send_sem=seg_send.at[k], recv_sem=seg_recv.at[k],
            device_id=(lax.rem(me + k, slabs), ray), device_id_type=MESH,
        )
        copy.start()
        copies.append(copy)
    for copy in copies:
        copy.wait()

    total = jnp.zeros((1, width), F32)
    pixels = jnp.zeros((3, width), F32)
    target = jnp.zeros((3, width), F32)
    shades, colors = [], []
    mine_shade = jnp.zeros((1, width), F32)
    for s in range(slabs):
        block = seg_all[s]
        shade = jnp.exp(total)
        pixels = pixels + shade * block[0:3]
        target = target + block[4:7]
        total = total + block[3:4]
        mine_shade = mine_shade + jnp.where(me == s, shade, 0.0)
        shades.append(shade)
        colors.append(block[0:3])
    clear = jnp.exp(total)
    pixels = pixels + clear
    pull = (2.0 * factor) * (pixels - target)
    d_log = clear * jnp.sum(pull, axis=0, keepdims=True)
    for s in range(slabs):
        term = shades[s] * jnp.sum(pull * colors[s], axis=0, keepdims=True)
        d_log = d_log + jnp.where(me < s, term, 0.0)
    d_color = mine_shade * pull
    pix_ref[...] = lax.dot_general(
        pixels, spread, NT, precision=lax.Precision.HIGHEST, preferred_element_type=F32
    )

    later = jnp.zeros((1, width), F32)
    d_out = [None] * SAMP
    for j in reversed(range(SAMP)):
        lanes = slice(j * width, (j + 1) * width)
        u = jnp.sum(d_color * tints[j], axis=0, keepdims=True)
        d_tau = after[j] * u - later - d_log
        later = later + weight[j] * u
        d0 = jnp.where(live[j], d_tau * delta * sigma_slope[:, lanes], 0.0)
        d_rgb = d_color * weight[j] * tints[j] * (1.0 - tints[j])
        d_out[j] = jnp.concatenate([d0, d_rgb, jnp.zeros((4, width), F32)], axis=0)
    d_out = jnp.concatenate(d_out, axis=1)
    do_hi, do_lo = split(d_out)
    wot_hi, wot_lo = split(wo.T)

    def last(at):
        lanes = pl.ds(at, chunk)
        hi = dh[1, 0:8, lanes]
        d = mm(wot_hi, hi) + mm(wot_lo, hi) + mm(wot_hi, dl[1, 0:8, lanes])
        hi, lo = split(d * sg[layers - 1, :, lanes])
        dh[0, :, lanes] = hi
        dl[0, :, lanes] = lo

    dh[1, 0:8, :] = do_hi
    dl[1, 0:8, :] = do_lo

    small = hid
    g[layers - 1, small:small + 32, :] = jnp.zeros((32, hid), F32)

    def head_grads():
        pair = mm_nt(jnp.concatenate([do_hi, do_lo], axis=0), hx[layers, hid:2 * hid, :])
        g_out = pair[0:8] + pair[8:16] + mm_nt(do_hi, hx[layers, 0:hid, :])
        g[layers - 1, small:small + 4, :] = g_out[0:4]
        ones = hx[0, 2 * hid:2 * hid + 16, :]
        row = mm_nt(ones, do_hi) + mm_nt(ones, do_lo)
        g[layers - 1, small + 7:small + 8, 0:8] = row[0:1, 0:8]

    chunks(last)

    def rows_of(b):
        return hid + 32 if b == layers - 1 else hid

    def piece(b):
        return rows_of(b) // 2 // PIECES

    def at_core(b, p, which):
        return pl.ds(pl.multiple_of(which * (rows_of(b) // 2) + p * piece(b), 8), piece(b))

    def stage_a(b, p):
        return pltpu.make_async_remote_copy(
            src_ref=g.at[b, at_core(b, p, 1 - core)],
            dst_ref=recv_a.at[b, pl.ds(p * piece(b), piece(b))],
            send_sem=a_send.at[b, p], recv_sem=a_recv.at[b, p],
            device_id=(me, other(1)), device_id_type=MESH,
        )

    def stage_b(b, i, p):
        rows = pl.ds(p * piece(b), piece(b))
        return pltpu.make_async_remote_copy(
            src_ref=part.at[b, i, rows], dst_ref=recv_b.at[b, i, rows],
            send_sem=b_send.at[b, i, p], recv_sem=b_recv.at[b, i, p],
            device_id=(me, other(1 << bits[i])), device_id_type=MESH,
        )

    def stage_c(b, p):
        rows = at_core(b, p, core)
        return pltpu.make_async_remote_copy(
            src_ref=fin.at[b, rows], dst_ref=fin.at[b, rows],
            send_sem=c_send.at[b, p], recv_sem=c_recv.at[b, p],
            device_id=(me, other(1)), device_id_type=MESH,
        )

    def send_on(b, i, p, value):
        if i < len(bits):
            part[b, i, p * piece(b):(p + 1) * piece(b), :] = value
            stage_b(b, i, p).start()
        else:
            fin[b, at_core(b, p, core), :] = value
            stage_c(b, p).start()

    def after_a(b):
        for p in range(PIECES):
            stage_a(b, p).wait()
            send_on(b, 0, p, g[b, at_core(b, p, core), :] + recv_a[b, p * piece(b):(p + 1) * piece(b), :])

    def after_b(b, i):
        for p in range(PIECES):
            rows = slice(p * piece(b), (p + 1) * piece(b))
            stage_b(b, i, p).wait()
            send_on(b, i + 1, p, part[b, i, rows, :] + recv_b[b, i, rows, :])

    for b in range(layers):
        l = layers - 1 - b
        slot = b % 2
        dz_hi, dz_lo = dh[slot], dl[slot]
        first = mm_nt(hx[l], dz_hi)
        second = mm_nt(hx[l, hid:2 * hid + 16], dz_lo)
        bias_row = first[2 * hid:2 * hid + 16] + second[hid:hid + 16]
        g[b, 0:hid, :] = first[0:hid] + first[hid:2 * hid] + second[0:hid]
        g[layers - 1, small + 4 + l:small + 5 + l, :] = bias_row[0:1]
        for p in range(PIECES):
            stage_a(b, p).start()
        if b == 0:
            head_grads()
        if l > 0:
            def back(at, l=l, slot=slot):
                lanes = pl.ds(at, chunk)
                both = mm(wn[l - 1], dh[slot, :, lanes])
                d = both[0:hid] + both[hid:2 * hid] + mm(wn[l - 1, 0:hid], dl[slot, :, lanes])
                hi, lo = split(d * sg[l - 1, :, lanes])
                dh[1 - slot, :, lanes] = hi
                dl[1 - slot, :, lanes] = lo
            chunks(back)
        after_a(b)
    for i in range(len(bits)):
        for b in range(layers):
            after_b(b, i)
    for b in range(layers):
        for p in range(PIECES):
            stage_c(b, p).wait()


def unpack(pix_in, fin, pix_ref, gin_ref, gmid_ref, gout_ref, ghid_ref, gbout_ref, sems):
    layers = fin.shape[0]
    hid = fin.shape[2]
    copies = []
    for l in range(layers):
        place = gin_ref.at[0] if l == 0 else gmid_ref.at[0, l - 1]
        copies.append(pltpu.make_async_copy(fin.at[layers - 1 - l, pl.ds(0, hid)], place, sems.at[l]))
    for copy in copies:
        copy.start()
    tail = fin[layers - 1, hid:hid + 16, :]
    gout_ref[0] = tail[0:4]
    ghid_ref[:, 0, :] = tail[4:4 + layers]
    gbout_ref[...] = tail[7:8, 0:4]
    pix_ref[:, 0, :] = pix_in[0:3, :]
    for copy in copies:
        copy.wait()


def solution(mesh):
    slabs, n_rays = mesh.shape["slab"], mesh.shape["rays"]

    def shards(geometry, entry, counts, targets, w_in, w_mid, w_out, b_hid, b_out, freqs):
        width = geometry.shape[2]
        own = targets.shape[2]
        n = SAMP * width
        hid = w_in.shape[2]
        mid = w_mid.shape[1]
        layers = mid + 1
        delta = 3.0 / (SAMP * slabs)
        factor = 1.0 / math.sqrt(3.0 * n_rays * slabs * own)
        more = max(1, sum(1 for b in range(1, 16) if (1 << b) < n_rays))
        half = (hid + 32) // 2
        shape = jax.ShapeDtypeStruct
        args = (
            geometry, entry, counts, targets, w_in, w_mid, w_out,
            jnp.transpose(b_hid, (1, 0, 2)), b_out, jnp.transpose(freqs, (1, 0, 2)),
        )
        vmem = pl.BlockSpec(memory_space=pltpu.VMEM)
        pixels, packed = pl.pallas_call(
            functools.partial(kernel, slabs, n_rays, delta, factor),
            out_shape=(pltpu.VMEM((3, own), F32), pltpu.VMEM((layers, hid + 32, hid), F32)),
            in_specs=[pl.BlockSpec(memory_space=pltpu.HBM)] * 10,
            out_specs=(vmem, vmem),
            scratch_shapes=[pltpu.VMEM(a.shape, a.dtype) for a in args] + [
                pltpu.VMEM((layers + 1, 2 * hid + 16, n), BF16),
                pltpu.VMEM((layers, hid, n), F32),
                pltpu.VMEM((2, hid, n), BF16),
                pltpu.VMEM((2, hid, n), BF16),
                pltpu.VMEM((layers, 2 * hid, hid), BF16),
                pltpu.VMEM((mid, 2 * hid, hid), BF16),
                pltpu.VMEM((slabs, 8, width), F32),
                pltpu.VMEM((layers, hid + 32, hid), F32),
                pltpu.VMEM((layers, half, hid), F32),
                pltpu.VMEM((layers, more, half, hid), F32),
                pltpu.VMEM((layers, more, half, hid), F32),
                pltpu.SemaphoreType.DMA((10,)),
                pltpu.SemaphoreType.DMA((slabs,)),
                pltpu.SemaphoreType.DMA((slabs,)),
                pltpu.SemaphoreType.DMA((layers, PIECES)),
                pltpu.SemaphoreType.DMA((layers, PIECES)),
                pltpu.SemaphoreType.DMA((layers, more, PIECES)),
                pltpu.SemaphoreType.DMA((layers, more, PIECES)),
                pltpu.SemaphoreType.DMA((layers, PIECES)),
                pltpu.SemaphoreType.DMA((layers, PIECES)),
            ],
            compiler_params=pltpu.CompilerParams(
                collective_id=0, has_side_effects=True, vmem_limit_bytes=58 * 1000 * 1024
            ),
        )(*args)
        hbm = pl.BlockSpec(memory_space=pltpu.HBM)
        outs = pl.pallas_call(
            unpack,
            out_shape=(
                shape((3, 1, own), F32),
                shape((1, 2 * freqs.shape[2], hid), F32),
                shape((1, mid, hid, hid), F32),
                shape((1, 4, hid), F32),
                shape((layers, 1, hid), F32),
                shape((1, 4), F32),
            ),
            in_specs=[vmem] * 2,
            out_specs=(vmem, hbm, hbm, vmem, vmem, vmem),
            scratch_shapes=[pltpu.SemaphoreType.DMA((layers,))],
            compiler_params=pltpu.CompilerParams(vmem_limit_bytes=8 << 20),
        )(pixels, packed)
        return outs[:4] + (jnp.transpose(outs[4], (1, 0, 2)), outs[5])

    in_specs = (
        P(None, "rays", None),
        P("slab", "rays", None),
        P("slab", "rays", None),
        P(None, "rays", "slab"),
        P("slab", None, None),
        P("slab", None, None, None),
        P("slab", None, None),
        P("slab", None, None),
        P("slab", None),
        P("slab", None, None),
    )
    out_specs = (
        P(None, "rays", "slab"),
        P("slab", None, None),
        P("slab", None, None, None),
        P("slab", None, None),
        P("slab", None, None),
        P("slab", None),
    )
    return jax.shard_map(shards, mesh=mesh, in_specs=in_specs, out_specs=out_specs, check_vma=False)
```
